32 devices in a mesh: tm: 2 (over x), gx: 4 (over y, core), gy: 4 (over z).
Axes of the slice: x: 2, y: 2, z: 4, core: 2. Of those that a mesh axis runs over, the one named last changes fastest.
Arguments:
- trajectory: float32 [4, 3, 128, 1024], P('tm', None, 'gy', 'gx'), may hold values from -3 to 3
- initial: float32 [3, 128, 1024], P(None, 'gy', 'gx'), may hold values from -3 to 3
Outputs:
- updated: float32 [4, 3, 128, 1024], P('tm', None, 'gy', 'gx')
- residual: float32 [4, 3, 128, 1024], P('tm', None, 'gy', 'gx')
The draws below stay inside these ranges and needn't reach their ends.
All inputs are finite; a program needn't handle non-finite values.
Results may differ from the reference program's by a relative error of at most 0.00023.
Values sent between devices are 32-bit elements; how exact they have to be, the bound alone decides.
No kernel may reach another device: no remote copies, remote signals or barrier semaphores. Data moves between devices by JAX's collectives and lax.ppermute only.
A program may use at most 64 MiB of HBM per device.

```python
import math
import jax
import jax.numpy as jnp
from jax import lax

CHEB = 6
NT = 4
NLAT = 128
NLON = 1024


def level_of(own_key, shape, pieces, low, largest):
    def one(position, blocks):
        heights = jax.random.uniform(jax.random.fold_in(jax.random.fold_in(own_key, 6), position), (blocks,), jnp.float32, low / len(pieces), largest / len(pieces))
        return jnp.repeat(jnp.exp(heights), shape[position] // blocks).reshape((-1,) + (1,) * (len(shape) - position - 1))

    loudness = one(*pieces[0])
    for cut in pieces[1:]:
        loudness = loudness * one(*cut)
    return loudness


def normal_values(rng, shape, width, reach, pieces=(), held_as=jnp.bfloat16):
    array = width * jax.random.normal(rng, shape, jnp.float32)
    if pieces:
        array = array * level_of(rng, shape, pieces, -0.22, 0.18)
    return jnp.clip(array, -reach, reach).astype(held_as)


def setup_inputs(seed: int = 0) -> dict:
    keys = jax.random.split(jax.random.key(seed), 3)
    return {
        "trajectory": normal_values(keys[0], (NT, 3, NLAT, NLON), 0.5, 3.0, ((0, 2), (2, 4), (3, 4)), jnp.float32),
        "initial": normal_values(keys[1], (3, NLAT, NLON), 0.5, 3.0, ((1, 4), (2, 4)), jnp.float32),
    }


courant_x = 1.5
courant_y = 1.5
coriolis_mean = 0.3
coriolis_slope = 0.4
circulant = 0.1
spectrum_edge = 5.0
highest = lax.Precision.HIGHEST


def along_lon(fields):
    return jnp.roll(fields, -1, -1) - jnp.roll(fields, 1, -1)


def along_lat(fields):
    return jnp.roll(fields, -1, -2) - jnp.roll(fields, 1, -2)


def coriolis(start, count, extent):
    latitude = (start + lax.iota(jnp.int32, count)).astype(jnp.float32)
    return (coriolis_mean + coriolis_slope * ((latitude + 0.5) / extent - 0.5))[:, None]


def wave(fields, rotation):
    height, eastward, northward = fields[..., 0, :, :], fields[..., 1, :, :], fields[..., 2, :, :]
    height_rate = courant_x * along_lon(eastward) + courant_y * along_lat(northward)
    east_rate = courant_x * along_lon(height) - rotation * northward
    north_rate = courant_y * along_lat(height) + rotation * eastward
    return jnp.stack([height_rate, east_rate, north_rate], axis=-3)


def advect(fields):
    height, eastward, northward = fields[..., 0, :, :], fields[..., 1, :, :], fields[..., 2, :, :]
    height_rate = courant_x * along_lon(height * eastward) + courant_y * along_lat(height * northward)
    east_rate = eastward * (courant_x * along_lon(eastward)) + northward * (courant_y * along_lat(eastward))
    north_rate = eastward * (courant_x * along_lon(northward)) + northward * (courant_y * along_lat(northward))
    return jnp.stack([height_rate, east_rate, north_rate], axis=-3)


def phase_table(rows, columns, total):
    products = (rows[:, None] * columns[None, :]) % total
    return (2.0 * math.pi / total) * products.astype(jnp.float32)


def time_weights(times, total, signed):
    return jnp.exp((signed * math.log(circulant) / total) * times.astype(jnp.float32))


def frequency_shift(frequency, total):
    factor = math.exp(math.log(circulant) / total)
    angle = (2.0 * math.pi / total) * frequency.astype(jnp.float32)
    return (1.0 - factor * jnp.cos(angle), factor * jnp.sin(angle))


def complex_times(first, second):
    return (first[0] * second[0] - first[1] * second[1], first[0] * second[1] + first[1] * second[0])


def complex_divide(first, second):
    denominator = second[0] * second[0] + second[1] * second[1]
    return ((first[0] * second[0] + first[1] * second[1]) / denominator,
            (first[1] * second[0] - first[0] * second[1]) / denominator)


def chebyshev(rhs, shift, operator):
    sigma = complex_divide(shift, (0.0, spectrum_edge))
    rho_old = complex_divide((1.0, 0.0), sigma)
    update = complex_divide(rhs, shift)
    solution = update
    for iteration in range(CHEB):
        turned = operator(solution)
        shifted = complex_times(shift, solution)
        misfit = (rhs[0] - (shifted[0] + turned[0]), rhs[1] - (shifted[1] + turned[1]))
        rho_new = complex_divide((1.0, 0.0), (2.0 * sigma[0] - rho_old[0], 2.0 * sigma[1] - rho_old[1]))
        carry_coef = complex_times(rho_new, rho_old)
        misfit_coef = complex_divide((2.0 * rho_new[0], 2.0 * rho_new[1]), (0.0, spectrum_edge))
        first_part = complex_times(carry_coef, update)
        second_part = complex_times(misfit_coef, misfit)
        update = (first_part[0] + second_part[0], first_part[1] + second_part[1])
        solution = (solution[0] + update[0], solution[1] + update[1])
        rho_old = rho_new
    return solution


def reference(trajectory, initial):
    total, fieldcount, nlat, nlon = trajectory.shape
    rotation = coriolis(0, nlat, nlat)
    previous = jnp.concatenate([initial[None], trajectory[:-1]], axis=0)
    residual = trajectory - previous + wave(trajectory, rotation) + advect(trajectory)
    times = lax.iota(jnp.int32, total)
    scaled = residual * time_weights(times, total, 1.0)[:, None, None, None]
    flat = scaled.reshape(total, -1)
    table = phase_table(times, times, total)
    cosines = jnp.cos(table)
    sines = jnp.sin(table)
    spec_re = jnp.dot(cosines, flat, precision=highest).reshape(trajectory.shape)
    spec_im = (-jnp.dot(sines, flat, precision=highest)).reshape(trajectory.shape)

    def wave_pair(couple):
        return (wave(couple[0], rotation), wave(couple[1], rotation))

    def solve_one(packed):
        rhs_re, rhs_im, frequency = packed
        shift = frequency_shift(frequency, total)
        return chebyshev((rhs_re, rhs_im), shift, wave_pair)

    sol_re, sol_im = lax.map(solve_one, (spec_re, spec_im, times))
    back = (jnp.dot(cosines, sol_re.reshape(total, -1), precision=highest)
            - jnp.dot(sines, sol_im.reshape(total, -1), precision=highest)) / total
    correction = back.reshape(trajectory.shape) * time_weights(times, total, -1.0)[:, None, None, None]
    return trajectory - correction, residual
```

```python
import cmath
import functools
import math

import jax
import jax.numpy as jnp
from jax import lax
from jax.experimental import pallas as pl
from jax.experimental.pallas import tpu as pltpu
from jax.sharding import PartitionSpec as P

CHEB = 6
COURANT = 1.5
CORIOLIS_MEAN = 0.3
CORIOLIS_SLOPE = 0.4
CIRCULANT = 0.1
SPECTRUM_EDGE = 5.0
HALO = 8
LANES = 128
SUBLANES = 8


def polynomials(total):
    factor = math.exp(math.log(CIRCULANT) / total)
    table = [[0.0] * (CHEB + 1) for _ in range(total)]
    for k in range(total):
        angle = 2.0 * math.pi * k / total
        shift = complex(1.0 - factor * math.cos(angle), factor * math.sin(angle))
        edge = 1j * SPECTRUM_EDGE
        sigma = shift / edge
        rho_old = 1.0 / sigma
        update = [1.0 / shift] + [0.0] * CHEB
        solved = list(update)
        for _ in range(CHEB):
            misfit = [-shift * solved[j] - (solved[j - 1] if j else -1.0) for j in range(CHEB + 1)]
            rho_new = 1.0 / (2.0 * sigma - rho_old)
            update = [rho_new * rho_old * a + 2.0 * rho_new / edge * b for a, b in zip(update, misfit)]
            solved = [a + b for a, b in zip(solved, update)]
            rho_old = rho_new
        for lag in range(total):
            turn = cmath.exp(1j * angle * lag) / total
            for j in range(CHEB + 1):
                table[lag][j] += (turn * solved[j]).real * COURANT**j
    return table


def pair_up(axis, odd):
    count = lax.axis_size(axis)
    first = range(1 if odd else 0, count, 2)
    return [pair for i in first for pair in ((i, (i + 1) % count), ((i + 1) % count, i))]


def with_steps(axis, pairs, by):
    times, count = lax.axis_size("tm"), lax.axis_size(axis)
    return [(t * count + a, (t + by) % times * count + b) for t in range(times) for a, b in pairs]


def dlon(q):
    return pltpu.roll(q, q.shape[1] - 1, 1) - pltpu.roll(q, 1, 1)


def dlat(q):
    return pltpu.roll(q, q.shape[0] - 1, 0) - pltpu.roll(q, 1, 0)


def pack_kernel(fields, traj, init, zr_even, zr_odd, xs, ys_even, ys_odd):
    width = traj.shape[-1]
    xs[:fields] = zr_even[:fields]
    xs[fields:] = zr_odd[:fields]
    gy_even = lax.axis_index("gy") % 2 == 0
    gx_even = lax.axis_index("gx") % 2 == 0
    lane = lax.broadcasted_iota(jnp.int32, (SUBLANES, LANES), 1)
    inner = traj.shape[-2] // SUBLANES

    def tile(rows, f, lanes):
        if rows == 0:
            return jnp.where(gy_even, zr_odd[f, :, lanes], zr_even[f, :, lanes])
        if rows == inner + 1:
            return jnp.where(gy_even, zr_even[f, :, lanes], zr_odd[f, :, lanes])
        at = pl.ds((rows - 1) * SUBLANES, SUBLANES)
        return traj[f // 3, f % 3, at, lanes] if f < fields else init[f - fields, at, lanes]

    for rows in range(inner + 2):
        first = jnp.zeros((SUBLANES, LANES), jnp.float32)
        last = first
        for f in range(fields + 3):
            here = (lane >= HALO * f) & (lane < HALO * (f + 1))
            head = tile(rows, f, pl.ds(0, LANES))
            tail = tile(rows, f, pl.ds(width - LANES, LANES))
            first = jnp.where(here, pltpu.roll(head, HALO * f, 1) if f else head, first)
            last = jnp.where(here, pltpu.roll(tail, HALO * (f + 1), 1), last)
        at = pl.ds(rows * SUBLANES, SUBLANES)
        ys_even[at, :] = jnp.where(gx_even, last, first)
        ys_odd[at, :] = jnp.where(gx_even, first, last)


def solve_kernel(times, steps, lags, *refs):
    fields = 3 * steps
    traj, init, zr_even, zr_odd, yr_even, yr_odd = refs[:6]
    others = refs[6 : 6 + 4 * (times - 1)]
    updated, residual, ext = refs[6 + 4 * (times - 1) :]
    rows_lat, width = traj.shape[-2:]
    inner = rows_lat // SUBLANES
    me, gy = lax.axis_index("tm"), lax.axis_index("gy")
    gy_even = gy % 2 == 0
    gx_even = lax.axis_index("gx") % 2 == 0
    lane = lax.broadcasted_iota(jnp.int32, (SUBLANES, LANES), 1)
    body = pl.ds(HALO, rows_lat)

    def place(f, own, own_at, even, odd, halo_at, pack_even, pack_odd, slot):
        ext[f, body, :width] = own[own_at]
        north, south = (even[halo_at], odd[halo_at])
        ext[f, :HALO, :width] = jnp.where(gy_even, south, north)
        ext[f, rows_lat + HALO :, :width] = jnp.where(gy_even, north, south)
        for rows in range(inner + 2):
            at = pl.ds(rows * SUBLANES, SUBLANES)
            east = jnp.where(gx_even, pack_even[at, :], pack_odd[at, :])
            west = jnp.where(gx_even, pack_odd[at, :], pack_even[at, :])
            east = pltpu.roll(east, LANES - HALO * slot, 1) if slot else east
            west = pltpu.roll(west, LANES - HALO * (slot + 1), 1)
            ext[f, at, width:] = jnp.where(lane < LANES // 2, east, west)

    for f in range(fields):
        place(f, traj, (f // 3, f % 3), zr_even, zr_odd, f, yr_even, yr_odd, f)
    for d in range(1, times):
        raw, xr, pack_even, pack_odd = others[4 * (d - 1) : 4 * d]
        for f in range(fields):
            place(d * fields + f, raw, (f // 3, f % 3), xr.at[:fields], xr.at[fields:], f, pack_even, pack_odd, f)
    for f in range(3):
        place(times * fields + f, init, f, zr_even, zr_odd, fields + f, yr_even, yr_odd, fields + f)

    shape = ext.shape[1:]
    nlat = rows_lat * lax.axis_size("gy")
    row = lax.broadcasted_iota(jnp.int32, shape, 0) + (gy * rows_lat - HALO)
    row = jnp.where(row < 0, row + nlat, jnp.where(row >= nlat, row - nlat, row))
    rotation = CORIOLIS_MEAN + CORIOLIS_SLOPE * ((row.astype(jnp.float32) + 0.5) / nlat - 0.5)

    total = times * steps
    first_field = times * fields
    for d in range(times):
        after = (d + 1) % times
        for l in range(steps):
            at = d * fields + 3 * l
            h, u, v = (ext[at + c] for c in range(3))
            if l:
                before = [ext[at - 3 + c] for c in range(3)]
            else:
                before = [
                    jnp.where(me == d, ext[first_field + c], ext[after * fields + fields - 3 + c]) for c in range(3)
                ]
            out = (
                h - before[0] + COURANT * (dlon(u + h * u) + dlat(v + h * v)),
                u - before[1] - rotation * v + COURANT * (dlon(h) + u * dlon(u) + v * dlat(u)),
                v - before[2] + rotation * u + COURANT * (dlat(h) + u * dlon(v) + v * dlat(v)),
            )
            if d == 0:
                for c in range(3):
                    residual[l, c] = out[c][HALO : HALO + rows_lat, :width]
            scale = jnp.where(me < d, jnp.float32(CIRCULANT), jnp.float32(1.0))
            for c in range(3):
                refs[-1][first_field + 3 + at + c] = out[c] * scale if d else out[c]

    def blend(n, j):
        sums = [None] * 3
        for d in range(times):
            for m in range(steps):
                lag = d * steps + n - m
                weight = lags[lag % total][j] * CIRCULANT ** (-lag / total)
                for c in range(3):
                    term = weight * ext[first_field + 3 + d * fields + 3 * m + c]
                    sums[c] = term if sums[c] is None else sums[c] + term
        return sums

    turn = rotation * (1.0 / COURANT)
    for n in range(steps):
        h, u, v = blend(n, CHEB)
        for j in range(CHEB - 1, -1, -1):
            add = blend(n, j)
            h, u, v = (
                add[0] + dlon(u) + dlat(v),
                add[1] + dlon(h) - turn * v,
                add[2] + dlat(h) + turn * u,
            )
        for c, value in enumerate((h, u, v)):
            updated[n, c] = traj[n, c] - value[HALO : HALO + rows_lat, :width]


def shards(trajectory, initial):
    steps, _, rows_lat, width = trajectory.shape
    times = lax.axis_size("tm")
    fields = 3 * steps
    lags = polynomials(times * steps)
    rows = rows_lat + 2 * HALO
    f32 = jnp.float32

    raws = [
        lax.ppermute(trajectory, "tm", [(t, (t + d) % times) for t in range(times)]) for d in range(1, times)
    ]
    flat = jnp.concatenate([trajectory.reshape(fields, rows_lat, width), initial], axis=0)
    gy_even = lax.axis_index("gy") % 2 == 0
    top, bottom = (flat[:, :HALO], flat[:, rows_lat - HALO :])
    zr_odd = lax.ppermute(jnp.where(gy_even, top, bottom), "gy", pair_up("gy", True))
    zr_even = lax.ppermute(jnp.where(gy_even, bottom, top), "gy", pair_up("gy", False))

    pack = jax.ShapeDtypeStruct((rows, LANES), f32)
    xs, ys_even, ys_odd = pl.pallas_call(
        functools.partial(pack_kernel, fields),
        out_shape=(jax.ShapeDtypeStruct((2 * fields, HALO, width), f32), pack, pack),
        name="pack_edges",
    )(trajectory, initial, zr_even, zr_odd)

    even, odd = (pair_up("gx", False), pair_up("gx", True))
    yr_odd = lax.ppermute(ys_odd, "gx", odd)
    yr_even = lax.ppermute(ys_even, "gx", even)
    others = []
    for d in range(1, times):
        others += [
            raws[d - 1],
            lax.ppermute(xs, "tm", [(t, (t + d) % times) for t in range(times)]),
            lax.ppermute(ys_even, ("tm", "gx"), with_steps("gx", even, d)),
            lax.ppermute(ys_odd, ("tm", "gx"), with_steps("gx", odd, d)),
        ]
    out = jax.ShapeDtypeStruct((steps, 3, rows_lat, width), f32)
    count = 2 * times * fields + 3
    updated, residual = pl.pallas_call(
        functools.partial(solve_kernel, times, steps, lags),
        out_shape=(out, out),
        scratch_shapes=[pltpu.VMEM((count, rows, width + LANES), f32)],
        name="solve_block",
    )(trajectory, initial, zr_even, zr_odd, yr_even, yr_odd, *others)
    return updated, residual


def solution(mesh):
    in_specs = (P("tm", None, "gy", "gx"), P(None, "gy", "gx"))
    out_specs = (P("tm", None, "gy", "gx"), P("tm", None, "gy", "gx"))
    return jax.shard_map(shards, mesh=mesh, in_specs=in_specs, out_specs=out_specs, check_vma=False)
```

```python
import cmath
import functools
import math
import operator

import jax
import jax.numpy as jnp
from jax import lax
from jax.experimental import pallas as pl
from jax.experimental.pallas import tpu as pltpu
from jax.sharding import PartitionSpec as P


CHEB = 6
COURANT = 1.5
CORIOLIS_MEAN = 0.3
CORIOLIS_SLOPE = 0.4
CIRCULANT = 0.1
SPECTRUM_EDGE = 5.0
REACH = CHEB + 1
HALO = 8
LANES = 128
VMEM_KEPT = 2**20
SUBLANES = 8


def polynomials(total):
    factor = math.exp(math.log(CIRCULANT) / total)
    table = [[0.0] * (CHEB + 1) for _ in range(total)]
    for k in range(total):
        angle = 2.0 * math.pi * k / total
        shift = complex(1.0 - factor * math.cos(angle), factor * math.sin(angle))
        edge = 1j * SPECTRUM_EDGE
        sigma = shift / edge
        rho_old = 1.0 / sigma
        update = [1.0 / shift] + [0.0] * CHEB
        solved = list(update)
        for _ in range(CHEB):
            misfit = [-shift * solved[j] - (solved[j - 1] if j else -1.0) for j in range(CHEB + 1)]
            rho_new = 1.0 / (2.0 * sigma - rho_old)
            update = [rho_new * rho_old * a + 2.0 * rho_new / edge * b for a, b in zip(update, misfit)]
            solved = [a + b for a, b in zip(solved, update)]
            rho_old = rho_new
        for lag in range(total):
            turn = cmath.exp(1j * angle * lag) / total
            for j in range(CHEB + 1):
                table[lag][j] += (turn * solved[j]).real * COURANT**j
    return table


def pair_up(axis, odd):
    count = lax.axis_size(axis)
    first = range(1 if odd else 0, count, 2)
    return [pair for i in first for pair in ((i, (i + 1) % count), ((i + 1) % count, i))]


def with_steps(axis, pairs, by):
    times, count = lax.axis_size("tm"), lax.axis_size(axis)
    return [(t * count + a, (t + by) % times * count + b) for t in range(times) for a, b in pairs]


def rotated(tiles, by):
    lane = lax.broadcasted_iota(jnp.int32, (SUBLANES, LANES), 1)
    turned = [pltpu.roll(tile, by % LANES, 1) for tile in tiles]
    if len(tiles) == 1:
        return turned
    edge = lane == (0 if by > 0 else LANES - 1)
    return [jnp.where(edge, turned[(w - by) % len(tiles)], turned[w]) for w in range(len(tiles))]


def dlon(tiles):
    return [east - west for east, west in zip(rotated(tiles, -1), rotated(tiles, 1))]


def around(load, q, tiles):
    north = load(q - 1) if q else [pltpu.roll(tile, 1, 0) for tile in load(tiles - 1)]
    south = load(q + 1) if q < tiles - 1 else [pltpu.roll(tile, SUBLANES - 1, 0) for tile in load(0)]
    return north, south


def dlat(load, q, tiles):
    north, south = around(load, q, tiles)
    return [s - n for s, n in zip(south, north)]


def dealt(ref, f, q):
    tiles = ref.shape[-2] // SUBLANES
    return [ref[f, w, pl.ds(q, SUBLANES, stride=tiles), :] for w in range(ref.shape[1])]


def gather_columns(tiles, width):
    lane = lax.broadcasted_iota(jnp.int32, (SUBLANES, LANES), 1)
    packed = jnp.zeros((SUBLANES, LANES), jnp.float32)
    half = LANES // 2
    for f, tile in enumerate(tiles):
        head = pltpu.roll(tile[:, :LANES], half + REACH * f, 1)
        tail = pltpu.roll(tile[:, width - LANES :], REACH * (f + 1), 1)
        at = lane - REACH * f
        packed = jnp.where((at >= 0) & (at < REACH), tail, packed)
        packed = jnp.where((at >= half) & (at < half + REACH), head, packed)
    return packed


def split_kernel(fields, traj, init, own, zs_even, zs_odd, packs):
    rows_lat, width = traj.shape[-2:]
    gy_even = lax.axis_index("gy") % 2 == 0
    for f in range(fields + 3):
        field = traj[f // 3, f % 3] if f < fields else init[f - fields]
        own[f] = field
        north, south = (field[:HALO], field[rows_lat - HALO :])
        zs_even[f] = jnp.where(gy_even, south, north)
        zs_odd[f] = jnp.where(gy_even, north, south)
    for rows in range(rows_lat // SUBLANES):
        at = pl.ds(rows * SUBLANES, SUBLANES)
        packs[at, :] = gather_columns([own.at[f, at] for f in range(fields + 3)], width)


def pack_kernel(fields, packs, zr_even, zr_odd, xs, ys):
    width = zr_even.shape[-1]
    gy_even = lax.axis_index("gy") % 2 == 0
    rows_lat = packs.shape[0]
    xs[:fields] = zr_even[:fields]
    xs[fields:] = zr_odd[:fields]
    even = gather_columns([zr_even.at[f] for f in range(fields + 3)], width)
    odd = gather_columns([zr_odd.at[f] for f in range(fields + 3)], width)
    ys[:HALO, :] = jnp.where(gy_even, odd, even)
    ys[HALO : HALO + rows_lat, :] = packs[...]
    ys[HALO + rows_lat :, :] = jnp.where(gy_even, even, odd)


def place(ext, base, own, even, odd):
    rows_lat, width = own[0].shape
    gy_even = lax.axis_index("gy") % 2 == 0
    for f, field in enumerate(own):
        for w in range(width // LANES):
            lanes = pl.ds(w * LANES, LANES)
            ext[base + f, w, pl.ds(HALO, rows_lat), :] = field[:, lanes]
            ext[base + f, w, pl.ds(0, HALO), :] = jnp.where(gy_even, odd[f, :, lanes], even[f, :, lanes])
            ext[base + f, w, pl.ds(rows_lat + HALO, HALO), :] = jnp.where(gy_even, even[f, :, lanes], odd[f, :, lanes])


def within(first, count, by=0):
    lane = lax.broadcasted_iota(jnp.int32, (SUBLANES, LANES), 1)
    return (lane - first - by) % LANES < count


def place_strips(strips, ext, count):
    tiles = ext.shape[1]
    for rows in range(ext.shape[2] // SUBLANES):
        rows = pl.ds(rows * SUBLANES, SUBLANES)
        for f in range(count):
            head = pltpu.roll(ext[f, 0, rows, :], LANES // 2 + REACH, 1)
            strips[f, rows, :] = jnp.where(within(LANES // 2 + REACH, 2 * REACH), head, ext[f, tiles - 1, rows, :])


def place_rim(rim, strips, at, count, slot, pack_even, pack_odd):
    half = LANES // 2
    lane = lax.broadcasted_iota(jnp.int32, (SUBLANES, LANES), 1)
    gx_even = lax.axis_index("gx") % 2 == 0
    from_odd = (lane < half) == gx_even
    outside = within(0, REACH) | within(half, REACH)
    for rows in range(strips.shape[1] // SUBLANES):
        rows = pl.ds(rows * SUBLANES, SUBLANES)
        both = jnp.where(from_odd, pack_odd[rows, :], pack_even[rows, :])
        for f in range(count):
            value = pltpu.roll(both, half - REACH * (slot + f), 1)
            rim[at + f, 0, rows, :] = jnp.where(outside, value, strips[at + f, rows, :])


def coriolis(q, rows_lat):
    gy = lax.axis_index("gy")
    nlat = rows_lat * lax.axis_size("gy")
    tiles = (rows_lat + 2 * HALO) // SUBLANES
    row = lax.broadcasted_iota(jnp.int32, (SUBLANES, LANES), 0) * tiles + (q - HALO) + gy * rows_lat
    row = jnp.where(row < 0, row + nlat, jnp.where(row >= nlat, row - nlat, row))
    return CORIOLIS_MEAN + CORIOLIS_SLOPE * ((row.astype(jnp.float32) + 0.5) / nlat - 0.5)


def tendency(load, q, tiles, rotation):
    h, u, v = (load(c, q) for c in range(3))

    def product(at):
        return [b + a * b for a, b in zip(load(0, at), load(2, at))]

    flow = dlon([b + a * b for a, b in zip(h, u)])
    east = [dlon(field) for field in (h, u, v)]
    north = [dlat(functools.partial(load, c), q, tiles) for c in range(3)]
    drift = dlat(product, q, tiles)
    out = ([], [], [])
    for w in range(len(h)):
        out[0].append(h[w] + COURANT * (flow[w] + drift[w]))
        out[1].append(u[w] - rotation * v[w] + COURANT * (east[0][w] + u[w] * east[1][w] + v[w] * north[1][w]))
        out[2].append(v[w] + rotation * u[w] + COURANT * (north[0][w] + u[w] * east[2][w] + v[w] * north[2][w]))
    return out


def horner(rates, weights, state, turn, write):
    outputs, (tiles, across) = range(len(weights)), rates.shape[1:3]

    def blend(n, j, c, q):
        terms = lambda t: (w[j] * rates[3 * i + c, q, t] for i, w in enumerate(weights[n]))
        return [functools.reduce(operator.add, terms(t)) for t in range(across)]

    for q in range(tiles):
        for n in outputs:
            for c in range(3):
                for t, value in enumerate(blend(n, CHEB, c, q)):
                    state[0, n, c, q, t] = value
    for j in range(CHEB - 1, -1, -1):
        now, later = ((CHEB - 1 - j) % 2, (CHEB - j) % 2)
        for q in range(tiles):
            for n in outputs:
                load = lambda c, at, n=n: [state[now, n, c, at, t] for t in range(across)]
                h, u, v = (load(c, q) for c in range(3))
                east_h, east_u = (dlon(h), dlon(u))
                north_h, north_v = (dlat(functools.partial(load, c), q, tiles) for c in (0, 2))
                add = [blend(n, j, c, q) for c in range(3)]
                new = (
                    [add[0][t] + (east_u[t] + north_v[t]) for t in range(across)],
                    [add[1][t] + (east_h[t] - turn[q] * v[t]) for t in range(across)],
                    [add[2][t] + (north_h[t] + turn[q] * u[t]) for t in range(across)],
                )
                for c in range(3):
                    if j:
                        for t in range(across):
                            state[later, n, c, q, t] = new[c][t]
                    else:
                        write(n, c, q, new[c])


def weights_of(lags, lag):
    return [w * CIRCULANT ** (-lag / len(lags)) for w in lags[lag % len(lags)]]


def put(scratch, f, q, values):
    tiles = scratch.shape[-2] // SUBLANES
    for w, value in enumerate(values):
        scratch[f, w, pl.ds(q, SUBLANES, stride=tiles), :] = value


def block_of(scratch, f, rows_lat):
    return jnp.concatenate([scratch[f, w, HALO : HALO + rows_lat] for w in range(scratch.shape[1])], axis=1)


def residuals(times, steps, ext, rates, rotation, write):
    fields, first = 3 * steps, 3 * steps * times
    tiles = rates.shape[1]
    me = lax.axis_index("tm")
    for d in range(times):
        scale = jnp.where(me < d, jnp.float32(CIRCULANT), jnp.float32(1.0))
        for l in range(steps):
            at = d * fields + 3 * l
            before = (at - 3) if l else ((d + 1) % times * fields + fields - 3)
            for q in range(tiles):
                out = tendency(lambda c, row: dealt(ext, at + c, row), q, tiles, rotation[q])
                for c in range(3):
                    prior = dealt(ext, before + c, q)
                    if l == 0:
                        prior = [jnp.where(me == d, a, b) for a, b in zip(dealt(ext, first + c, q), prior)]
                    values = [a - b for a, b in zip(out[c], prior)]
                    if d == 0:
                        write(l, c, q, values)
                    for t, value in enumerate(values):
                        rates[at + c, q, t] = scale * value if d else value


def weights_for(times, steps, lags):
    return [
        [weights_of(lags, d * steps + n - m) for d in range(times) for m in range(steps)] for n in range(steps)
    ]


def block_kernel(times, steps, lags, own, zr_even, zr_odd, *refs):
    fields = 3 * steps
    others = refs[: 2 * (times - 1)]
    strips, part, residual, ext, rates, state, scratch = refs[2 * (times - 1) :]
    rows_lat = own.shape[-2]
    place(ext, 0, [own.at[f] for f in range(fields)], zr_even.at[:fields], zr_odd.at[:fields])
    for d in range(1, times):
        raw, xr = others[2 * (d - 1) : 2 * d]
        blocks = [raw.at[f // 3, f % 3] for f in range(fields)]
        place(ext, d * fields, blocks, xr.at[:fields], xr.at[fields:])
    place(ext, times * fields, [own.at[fields + c] for c in range(3)], zr_even.at[fields:], zr_odd.at[fields:])
    rotation = [coriolis(q, rows_lat) for q in range(rates.shape[1])]
    residuals(times, steps, ext, rates, rotation, lambda l, c, q, values: put(scratch, 3 * l + c, q, values))
    for l in range(steps):
        for c in range(3):
            residual[l, c] = block_of(scratch, 3 * l + c, rows_lat)
    place_strips(strips, ext, times * fields + 3)
    turn = [r * (1.0 / COURANT) for r in rotation]
    weights = weights_for(times, steps, lags)
    horner(rates, weights, state, turn, lambda n, c, q, values: put(scratch, fields + 3 * n + c, q, values))
    for n in range(steps):
        for c in range(3):
            part[n, c] = block_of(scratch, fields + 3 * n + c, rows_lat)


APART = 4 * REACH


def rim_kernel(times, steps, lags, own, strips, part, part_residual, yr_even, yr_odd, *refs):
    fields, half = 3 * steps, LANES // 2
    packs = refs[: 2 * (times - 1)]
    updated, residual, rim, rates, state, scratch = refs[2 * (times - 1) :]
    rows_lat, width = own.shape[-2:]
    tiles = rates.shape[1]
    place_rim(rim, strips, 0, fields, 0, yr_even, yr_odd)
    place_rim(rim, strips, times * fields, 3, fields, yr_even, yr_odd)
    for d in range(1, times):
        place_rim(rim, strips, d * fields, fields, 0, *packs[2 * (d - 1) : 2 * d])
    rotation = [coriolis(q, rows_lat) for q in range(tiles)]
    residuals(times, steps, rim, rates, rotation, lambda l, c, q, values: put(scratch, 3 * l + c, q, values))
    lane = lax.broadcasted_iota(jnp.int32, (rows_lat, LANES), 1)

    def merged(value, strip, by):
        tail = pltpu.roll(strip, LANES - by, 1) if by else strip
        head = pltpu.roll(strip, half - REACH - by, 1)
        value = [value[:, w * LANES : (w + 1) * LANES] for w in range(width // LANES)]
        value[0] = jnp.where(lane < REACH, head, value[0])
        value[-1] = jnp.where(lane >= LANES - REACH, tail, value[-1])
        return jnp.concatenate(value, axis=1)

    for l in range(steps):
        for c in range(3):
            residual[l, c] = merged(part_residual[l, c], block_of(scratch, 3 * l + c, rows_lat), 0)

    second = within(LANES - 2 * REACH, 3 * REACH, APART) | within(half, 3 * REACH, APART)
    for f in range(times * fields):
        for q in range(tiles):
            rates[f, q, 0] = jnp.where(second, pltpu.roll(rates[f, q, 0], APART, 1), rates[f, q, 0])
    turn = [r * (1.0 / COURANT) for r in rotation]
    plain = weights_for(times, steps, lags)
    for n in range(0, steps, 2):
        pair = [
            [[jnp.where(second, b, a) for a, b in zip(*both)] for both in zip(plain[n], plain[min(n + 1, steps - 1)])]
        ]
        horner(rates, pair, state, turn, lambda _, c, q, values: put(scratch, c, q, values))
        for c in range(3):
            strip = block_of(scratch, c, rows_lat)
            for m in range(n, min(n + 2, steps)):
                updated[m, c] = own[3 * m + c] - merged(part[m, c], strip, (m - n) * APART)


def step(trajectory, initial):
    steps, _, rows_lat, width = trajectory.shape
    times = lax.axis_size("tm")
    fields = 3 * steps
    lags = polynomials(times * steps)

    def vmem(*shape):
        return pltpu.VMEM(shape, jnp.float32)

    rows, across = (rows_lat + 2 * HALO, width // LANES)
    known = times * fields

    def hbm(*shape):
        return jax.ShapeDtypeStruct(shape, jnp.float32)

    fits = 4 * known * rows * width <= VMEM_KEPT
    near = vmem if fits else hbm

    def kept(*arrays):
        return [pltpu.with_memory_space_constraint(array, pltpu.VMEM) if fits else array for array in arrays]

    own, zs_even, zs_odd, packs = pl.pallas_call(
        functools.partial(split_kernel, fields),
        out_shape=(
            near(fields + 3, rows_lat, width),
            near(fields + 3, HALO, width),
            near(fields + 3, HALO, width),
            near(rows_lat, LANES),
        ),
        name="split_edges",
    )(trajectory, initial)
    zr_odd = lax.ppermute(zs_odd, "gy", pair_up("gy", True))
    zr_even = lax.ppermute(zs_even, "gy", pair_up("gy", False))
    shifts = [[(t, (t + d) % times) for t in range(times)] for d in range(times)]
    raws = [lax.ppermute(trajectory, "tm", shifts[d]) for d in range(1, times)]

    xs, ys = pl.pallas_call(
        functools.partial(pack_kernel, fields),
        out_shape=(near(2 * fields, HALO, width), near(rows, LANES)),
        name="pack_edges",
    )(*kept(packs, zr_even, zr_odd))

    even, odd = (pair_up("gx", False), pair_up("gx", True))
    x_rows = [lax.ppermute(xs, "tm", shifts[d]) for d in range(1, times)]
    packs = [lax.ppermute(ys, "gx", even), lax.ppermute(ys, "gx", odd)]
    for d in range(1, times):
        packs.append(lax.ppermute(ys, ("tm", "gx"), with_steps("gx", even, d)))
        packs.append(lax.ppermute(ys, ("tm", "gx"), with_steps("gx", odd, d)))

    def dealt_out(count, tiles):
        return vmem(count, rows // SUBLANES, tiles, SUBLANES, LANES)

    def working(outputs, scratch, tiles):
        state = vmem(2, outputs, 3, rows // SUBLANES, tiles, SUBLANES, LANES)
        return [dealt_out(known, tiles), state, vmem(scratch, tiles, rows, LANES)]

    strips, part, part_residual = pl.pallas_call(
        functools.partial(block_kernel, times, steps, lags),
        out_shape=(
            near(known + 3, rows, LANES),
            near(steps, 3, rows_lat, width),
            near(steps, 3, rows_lat, width),
        ),
        scratch_shapes=[vmem(known + 3, across, rows, LANES)] + working(steps, 2 * fields, across),
        name="block_part",
    )(*kept(own, zr_even, zr_odd, *(each for both in zip(raws, x_rows) for each in both)))
    updated, residual = pl.pallas_call(
        functools.partial(rim_kernel, times, steps, lags),
        out_shape=(hbm(steps, 3, rows_lat, width), hbm(steps, 3, rows_lat, width)),
        scratch_shapes=[vmem(known + 3, 1, rows, LANES)] + working(1, fields, 1),
        name="rim_part",
    )(*kept(own, strips, part, part_residual, *packs))
    return updated, residual


def solution(mesh):
    in_specs = (P("tm", None, "gy", "gx"), P(None, "gy", "gx"))
    out_specs = (P("tm", None, "gy", "gx"), P("tm", None, "gy", "gx"))
    return jax.shard_map(step, mesh=mesh, in_specs=in_specs, out_specs=out_specs, check_vma=False)
```

```python
import cmath
import functools
import math
import operator

import jax
import jax.numpy as jnp
from jax import lax
from jax.experimental import pallas as pl
from jax.experimental.pallas import tpu as pltpu
from jax.sharding import PartitionSpec as P


CHEB = 6
COURANT = 1.5
CORIOLIS_MEAN = 0.3
CORIOLIS_SLOPE = 0.4
CIRCULANT = 0.1
SPECTRUM_EDGE = 5.0
REACH = CHEB + 1
HALO = 8
LANES = 128
VMEM_KEPT = 2**20
SUBLANES = 8


def polynomials(total):
    factor = math.exp(math.log(CIRCULANT) / total)
    table = [[0.0] * (CHEB + 1) for _ in range(total)]
    for k in range(total):
        angle = 2.0 * math.pi * k / total
        shift = complex(1.0 - factor * math.cos(angle), factor * math.sin(angle))
        edge = 1j * SPECTRUM_EDGE
        sigma = shift / edge
        rho_old = 1.0 / sigma
        update = [1.0 / shift] + [0.0] * CHEB
        solved = list(update)
        for _ in range(CHEB):
            misfit = [-shift * solved[j] - (solved[j - 1] if j else -1.0) for j in range(CHEB + 1)]
            rho_new = 1.0 / (2.0 * sigma - rho_old)
            update = [rho_new * rho_old * a + 2.0 * rho_new / edge * b for a, b in zip(update, misfit)]
            solved = [a + b for a, b in zip(solved, update)]
            rho_old = rho_new
        for lag in range(total):
            turn = cmath.exp(1j * angle * lag) / total
            for j in range(CHEB + 1):
                table[lag][j] += (turn * solved[j]).real * COURANT**j
    return table


def pair_up(axis, odd):
    count = lax.axis_size(axis)
    first = range(1 if odd else 0, count, 2)
    return [pair for i in first for pair in ((i, (i + 1) % count), ((i + 1) % count, i))]


def with_steps(axis, pairs, by):
    times, count = lax.axis_size("tm"), lax.axis_size(axis)
    return [(t * count + a, (t + by) % times * count + b) for t in range(times) for a, b in pairs]


def rotated(tiles, by):
    lane = lax.broadcasted_iota(jnp.int32, (SUBLANES, LANES), 1)
    turned = [pltpu.roll(tile, by % LANES, 1) for tile in tiles]
    if len(tiles) == 1:
        return turned
    edge = lane == (0 if by > 0 else LANES - 1)
    return [jnp.where(edge, turned[(w - by) % len(tiles)], turned[w]) for w in range(len(tiles))]


def dlon(tiles):
    return [east - west for east, west in zip(rotated(tiles, -1), rotated(tiles, 1))]


def around(load, q, tiles):
    north = load(q - 1) if q else [pltpu.roll(tile, 1, 0) for tile in load(tiles - 1)]
    south = load(q + 1) if q < tiles - 1 else [pltpu.roll(tile, SUBLANES - 1, 0) for tile in load(0)]
    return north, south


def dlat(load, q, tiles):
    north, south = around(load, q, tiles)
    return [s - n for s, n in zip(south, north)]


def dealt(ref, f, q):
    tiles = ref.shape[-2] // SUBLANES
    return [ref[f, w, pl.ds(q, SUBLANES, stride=tiles), :] for w in range(ref.shape[1])]


def gather_columns(tiles, width):
    lane = lax.broadcasted_iota(jnp.int32, (SUBLANES, LANES), 1)
    packed = jnp.zeros((SUBLANES, LANES), jnp.float32)
    half = LANES // 2
    for f, tile in enumerate(tiles):
        head = pltpu.roll(tile[:, :LANES], half + REACH * f, 1)
        tail = pltpu.roll(tile[:, width - LANES :], REACH * (f + 1), 1)
        at = lane - REACH * f
        packed = jnp.where((at >= 0) & (at < REACH), tail, packed)
        packed = jnp.where((at >= half) & (at < half + REACH), head, packed)
    return packed


def edge_kernel(steps, traj, init, zs_even, zs_odd, sems):
    rows_lat = traj.shape[-2]
    gy_even = lax.axis_index("gy") % 2 == 0
    copies = []
    for side, (target, south) in enumerate(((zs_even, gy_even), (zs_odd, jnp.logical_not(gy_even)))):
        rows = pl.ds(pl.multiple_of(jnp.where(south, rows_lat - HALO, 0), SUBLANES), HALO)
        for l in range(steps + 1):
            source = traj.at[l, :, rows, :] if l < steps else init.at[:, rows, :]
            copies.append(pltpu.make_async_copy(source, target.at[pl.ds(3 * l, 3)], sems.at[side, l]))
    for copy in copies:
        copy.start()
    for copy in copies:
        copy.wait()


def split_kernel(fields, traj, init, own, packs):
    rows_lat, width = traj.shape[-2:]
    for f in range(fields + 3):
        own[f] = traj[f // 3, f % 3] if f < fields else init[f - fields]
    for rows in range(rows_lat // SUBLANES):
        at = pl.ds(rows * SUBLANES, SUBLANES)
        packs[at, :] = gather_columns([own.at[f, at] for f in range(fields + 3)], width)


def other_pack_kernel(fields, *refs):
    own, others, packs = refs[0], refs[1:-1], refs[-1]
    gy_even = lax.axis_index("gy") % 2 == 0
    packs[0] = own[...]
    for d in range(len(others) // 3):
        raw, xr_even, xr_odd = others[3 * d : 3 * d + 3]
        rows_lat, width = raw.shape[-2:]
        even = gather_columns([xr_even.at[f] for f in range(fields)], width)
        odd = gather_columns([xr_odd.at[f] for f in range(fields)], width)
        packs[d + 1, :HALO, :] = jnp.where(gy_even, odd, even)
        packs[d + 1, HALO + rows_lat :, :] = jnp.where(gy_even, even, odd)
        for rows in range(rows_lat // SUBLANES):
            at = pl.ds(rows * SUBLANES, SUBLANES)
            tiles = [raw.at[f // 3, f % 3, at] for f in range(fields)]
            packs[d + 1, pl.ds(HALO + rows * SUBLANES, SUBLANES), :] = gather_columns(tiles, width)


def pack_kernel(fields, packs, zr_even, zr_odd, ys):
    width = zr_even.shape[-1]
    gy_even = lax.axis_index("gy") % 2 == 0
    rows_lat = packs.shape[0]
    even = gather_columns([zr_even.at[f] for f in range(fields + 3)], width)
    odd = gather_columns([zr_odd.at[f] for f in range(fields + 3)], width)
    ys[:HALO, :] = jnp.where(gy_even, odd, even)
    ys[HALO : HALO + rows_lat, :] = packs[...]
    ys[HALO + rows_lat :, :] = jnp.where(gy_even, even, odd)


def place(ext, base, own, even, odd):
    rows_lat, width = own[0].shape
    gy_even = lax.axis_index("gy") % 2 == 0
    for f, field in enumerate(own):
        for w in range(width // LANES):
            lanes = pl.ds(w * LANES, LANES)
            ext[base + f, w, pl.ds(HALO, rows_lat), :] = field[:, lanes]
            ext[base + f, w, pl.ds(0, HALO), :] = jnp.where(gy_even, odd[f, :, lanes], even[f, :, lanes])
            ext[base + f, w, pl.ds(rows_lat + HALO, HALO), :] = jnp.where(gy_even, even[f, :, lanes], odd[f, :, lanes])


def within(first, count, by=0):
    lane = lax.broadcasted_iota(jnp.int32, (SUBLANES, LANES), 1)
    return (lane - first - by) % LANES < count


def place_strips(strips, ext, count):
    tiles = ext.shape[1]
    for rows in range(ext.shape[2] // SUBLANES):
        rows = pl.ds(rows * SUBLANES, SUBLANES)
        for f in range(count):
            head = pltpu.roll(ext[f, 0, rows, :], LANES // 2 + REACH, 1)
            strips[f, rows, :] = jnp.where(within(LANES // 2 + REACH, 2 * REACH), head, ext[f, tiles - 1, rows, :])


def place_rim(rim, strips, at, count, slot, pack_even, pack_odd):
    half = LANES // 2
    lane = lax.broadcasted_iota(jnp.int32, (SUBLANES, LANES), 1)
    gx_even = lax.axis_index("gx") % 2 == 0
    from_odd = (lane < half) == gx_even
    outside = within(0, REACH) | within(half, REACH)
    for rows in range(strips.shape[1] // SUBLANES):
        rows = pl.ds(rows * SUBLANES, SUBLANES)
        both = jnp.where(from_odd, pack_odd[rows, :], pack_even[rows, :])
        for f in range(count):
            value = pltpu.roll(both, half - REACH * (slot + f), 1)
            rim[at + f, 0, rows, :] = jnp.where(outside, value, strips[at + f, rows, :])


def coriolis(q, rows_lat):
    gy = lax.axis_index("gy")
    nlat = rows_lat * lax.axis_size("gy")
    tiles = (rows_lat + 2 * HALO) // SUBLANES
    row = lax.broadcasted_iota(jnp.int32, (SUBLANES, LANES), 0) * tiles + (q - HALO) + gy * rows_lat
    row = jnp.where(row < 0, row + nlat, jnp.where(row >= nlat, row - nlat, row))
    return CORIOLIS_MEAN + CORIOLIS_SLOPE * ((row.astype(jnp.float32) + 0.5) / nlat - 0.5)


def tendency(load, q, tiles, rotation):
    h, u, v = (load(c, q) for c in range(3))

    def product(at):
        return [b + a * b for a, b in zip(load(0, at), load(2, at))]

    flow = dlon([b + a * b for a, b in zip(h, u)])
    east = [dlon(field) for field in (h, u, v)]
    north = [dlat(functools.partial(load, c), q, tiles) for c in range(3)]
    drift = dlat(product, q, tiles)
    out = ([], [], [])
    for w in range(len(h)):
        out[0].append(h[w] + COURANT * (flow[w] + drift[w]))
        out[1].append(u[w] - rotation * v[w] + COURANT * (east[0][w] + u[w] * east[1][w] + v[w] * north[1][w]))
        out[2].append(v[w] + rotation * u[w] + COURANT * (north[0][w] + u[w] * east[2][w] + v[w] * north[2][w]))
    return out


def horner(rates, weights, state, turn, write):
    outputs, (tiles, across) = range(len(weights)), rates.shape[1:3]

    def blend(n, j, c, q):
        terms = lambda t: (w[j] * rates[3 * i + c, q, t] for i, w in enumerate(weights[n]))
        return [functools.reduce(operator.add, terms(t)) for t in range(across)]

    for q in range(tiles):
        for n in outputs:
            for c in range(3):
                for t, value in enumerate(blend(n, CHEB, c, q)):
                    state[0, n, c, q, t] = value
    for j in range(CHEB - 1, -1, -1):
        now, later = ((CHEB - 1 - j) % 2, (CHEB - j) % 2)
        for q in range(tiles):
            for n in outputs:
                load = lambda c, at, n=n: [state[now, n, c, at, t] for t in range(across)]
                h, u, v = (load(c, q) for c in range(3))
                east_h, east_u = (dlon(h), dlon(u))
                north_h, north_v = (dlat(functools.partial(load, c), q, tiles) for c in (0, 2))
                add = [blend(n, j, c, q) for c in range(3)]
                new = (
                    [add[0][t] + (east_u[t] + north_v[t]) for t in range(across)],
                    [add[1][t] + (east_h[t] - turn[q] * v[t]) for t in range(across)],
                    [add[2][t] + (north_h[t] + turn[q] * u[t]) for t in range(across)],
                )
                for c in range(3):
                    if j:
                        for t in range(across):
                            state[later, n, c, q, t] = new[c][t]
                    else:
                        write(n, c, q, new[c])


def weights_of(lags, lag):
    return [w * CIRCULANT ** (-lag / len(lags)) for w in lags[lag % len(lags)]]


def put(scratch, f, q, values):
    tiles = scratch.shape[-2] // SUBLANES
    for w, value in enumerate(values):
        scratch[f, w, pl.ds(q, SUBLANES, stride=tiles), :] = value


def block_of(scratch, f, rows_lat):
    return jnp.concatenate([scratch[f, w, HALO : HALO + rows_lat] for w in range(scratch.shape[1])], axis=1)


def residuals(times, steps, ext, rates, rotation, write):
    fields, first = 3 * steps, 3 * steps * times
    tiles = rates.shape[1]
    me = lax.axis_index("tm")
    for d in range(times):
        scale = jnp.where(me < d, jnp.float32(CIRCULANT), jnp.float32(1.0))
        for l in range(steps):
            at = d * fields + 3 * l
            before = (at - 3) if l else ((d + 1) % times * fields + fields - 3)
            for q in range(tiles):
                out = tendency(lambda c, row: dealt(ext, at + c, row), q, tiles, rotation[q])
                for c in range(3):
                    prior = dealt(ext, before + c, q)
                    if l == 0:
                        prior = [jnp.where(me == d, a, b) for a, b in zip(dealt(ext, first + c, q), prior)]
                    values = [a - b for a, b in zip(out[c], prior)]
                    if d == 0:
                        write(l, c, q, values)
                    for t, value in enumerate(values):
                        rates[at + c, q, t] = scale * value if d else value


def weights_for(times, steps, lags):
    return [
        [weights_of(lags, d * steps + n - m) for d in range(times) for m in range(steps)] for n in range(steps)
    ]


def block_kernel(times, steps, lags, own, zr_even, zr_odd, *refs):
    fields = 3 * steps
    others = refs[: 3 * (times - 1)]
    strips, part, residual, ext, rates, state, scratch = refs[3 * (times - 1) :]
    rows_lat = own.shape[-2]
    place(ext, 0, [own.at[f] for f in range(fields)], zr_even.at[:fields], zr_odd.at[:fields])
    for d in range(1, times):
        raw, xr_even, xr_odd = others[3 * (d - 1) : 3 * d]
        blocks = [raw.at[f // 3, f % 3] for f in range(fields)]
        place(ext, d * fields, blocks, xr_even, xr_odd)
    place(ext, times * fields, [own.at[fields + c] for c in range(3)], zr_even.at[fields:], zr_odd.at[fields:])
    rotation = [coriolis(q, rows_lat) for q in range(rates.shape[1])]
    residuals(times, steps, ext, rates, rotation, lambda l, c, q, values: put(scratch, 3 * l + c, q, values))
    for l in range(steps):
        for c in range(3):
            residual[l, c] = block_of(scratch, 3 * l + c, rows_lat)
    place_strips(strips, ext, times * fields + 3)
    turn = [r * (1.0 / COURANT) for r in rotation]
    weights = weights_for(times, steps, lags)
    horner(rates, weights, state, turn, lambda n, c, q, values: put(scratch, fields + 3 * n + c, q, values))
    for n in range(steps):
        for c in range(3):
            part[n, c] = block_of(scratch, fields + 3 * n + c, rows_lat)


APART = 4 * REACH


def rim_kernel(times, steps, lags, own, strips, part, part_residual, yr_even, yr_odd, *refs):
    fields, half = 3 * steps, LANES // 2
    updated, residual, rim, rates, state, scratch, ready, sems = refs[times - 1 :]
    rows_lat, width = own.shape[-2:]
    tiles = rates.shape[1]
    place_rim(rim, strips, 0, fields, 0, yr_even.at[0], yr_odd)
    place_rim(rim, strips, times * fields, 3, fields, yr_even.at[0], yr_odd)
    for d in range(1, times):
        place_rim(rim, strips, d * fields, fields, 0, yr_even.at[d], refs[d - 1])
    rotation = [coriolis(q, rows_lat) for q in range(tiles)]
    residuals(times, steps, rim, rates, rotation, lambda l, c, q, values: put(scratch, 3 * l + c, q, values))
    lane = lax.broadcasted_iota(jnp.int32, (rows_lat, LANES), 1)

    def merged(value, strip, by):
        tail = pltpu.roll(strip, LANES - by, 1) if by else strip
        head = pltpu.roll(strip, half - REACH - by, 1)
        value = [value[:, w * LANES : (w + 1) * LANES] for w in range(width // LANES)]
        value[0] = jnp.where(lane < REACH, head, value[0])
        value[-1] = jnp.where(lane >= LANES - REACH, tail, value[-1])
        return jnp.concatenate(value, axis=1)

    copies = []
    for l in range(steps):
        for c in range(3):
            ready[l, c] = merged(part_residual[l, c], block_of(scratch, 3 * l + c, rows_lat), 0)
            copies.append(pltpu.make_async_copy(ready.at[l, c], residual.at[l, c], sems.at[l, c]))
            copies[-1].start()

    second = within(LANES - 2 * REACH, 3 * REACH, APART) | within(half, 3 * REACH, APART)
    for f in range(times * fields):
        for q in range(tiles):
            rates[f, q, 0] = jnp.where(second, pltpu.roll(rates[f, q, 0], APART, 1), rates[f, q, 0])
    turn = [r * (1.0 / COURANT) for r in rotation]
    plain = weights_for(times, steps, lags)
    for n in range(0, steps, 2):
        pair = [
            [[jnp.where(second, b, a) for a, b in zip(*both)] for both in zip(plain[n], plain[min(n + 1, steps - 1)])]
        ]
        horner(rates, pair, state, turn, lambda _, c, q, values: put(scratch, c, q, values))
        for c in range(3):
            strip = block_of(scratch, c, rows_lat)
            for m in range(n, min(n + 2, steps)):
                ready[steps + m, c] = own[3 * m + c] - merged(part[m, c], strip, (m - n) * APART)
                copies.append(pltpu.make_async_copy(ready.at[steps + m, c], updated.at[m, c], sems.at[steps + m, c]))
                copies[-1].start()
    for copy in copies:
        copy.wait()


def step(trajectory, initial):
    steps, _, rows_lat, width = trajectory.shape
    times = lax.axis_size("tm")
    fields = 3 * steps
    lags = polynomials(times * steps)

    def vmem(*shape):
        return pltpu.VMEM(shape, jnp.float32)

    rows, across = (rows_lat + 2 * HALO, width // LANES)
    known = times * fields

    def hbm(*shape):
        return jax.ShapeDtypeStruct(shape, jnp.float32)

    fits = 4 * known * rows * width <= VMEM_KEPT
    near = vmem if fits else hbm

    def kept(*arrays):
        return [pltpu.with_memory_space_constraint(array, pltpu.VMEM) if fits else array for array in arrays]

    zs_even, zs_odd = pl.pallas_call(
        functools.partial(edge_kernel, steps),
        in_specs=[pl.BlockSpec(memory_space=pl.ANY)] * 2,
        out_shape=(near(fields + 3, HALO, width), near(fields + 3, HALO, width)),
        scratch_shapes=[pltpu.SemaphoreType.DMA((2, steps + 1))],
        name="edge_rows",
    )(trajectory, initial)
    zr_odd = lax.ppermute(zs_odd, "gy", pair_up("gy", True))
    zr_even = lax.ppermute(zs_even, "gy", pair_up("gy", False))
    own, packs = pl.pallas_call(
        functools.partial(split_kernel, fields),
        out_shape=(near(fields + 3, rows_lat, width), near(rows_lat, LANES)),
        name="split_block",
    )(trajectory, initial)
    shifts = [[(t, (t + d) % times) for t in range(times)] for d in range(times)]
    raws = [lax.ppermute(trajectory, "tm", shifts[d]) for d in range(1, times)]

    ys = pl.pallas_call(
        functools.partial(pack_kernel, fields),
        out_shape=near(rows, LANES),
        name="pack_edges",
    )(*kept(packs, zr_even, zr_odd))

    even, odd = (pair_up("gx", False), pair_up("gx", True))
    xr_even = [lax.ppermute(zr_even[:fields], "tm", shifts[d]) for d in range(1, times)]
    xr_odd = [lax.ppermute(zr_odd[:fields], "tm", shifts[d]) for d in range(1, times)]
    odds = [lax.ppermute(ys, ("tm", "gx"), with_steps("gx", odd, d)) for d in range(1, times)]
    odds.insert(0, lax.ppermute(ys, "gx", odd))
    known_of = [each for both in zip(raws, xr_even, xr_odd) for each in both]
    ys_all = pl.pallas_call(
        functools.partial(other_pack_kernel, fields),
        out_shape=near(times, rows, LANES),
        name="pack_others",
    )(*kept(ys, *known_of))
    evens = lax.ppermute(ys_all, "gx", even)

    def dealt_out(count, tiles):
        return vmem(count, rows // SUBLANES, tiles, SUBLANES, LANES)

    def working(outputs, scratch, tiles):
        state = vmem(2, outputs, 3, rows // SUBLANES, tiles, SUBLANES, LANES)
        return [dealt_out(known, tiles), state, vmem(scratch, tiles, rows, LANES)]

    strips, part, part_residual = pl.pallas_call(
        functools.partial(block_kernel, times, steps, lags),
        out_shape=(
            near(known + 3, rows, LANES),
            near(steps, 3, rows_lat, width),
            near(steps, 3, rows_lat, width),
        ),
        scratch_shapes=[vmem(known + 3, across, rows, LANES)] + working(steps, 2 * fields, across),
        name="block_part",
    )(*kept(own, zr_even, zr_odd, *known_of))
    updated, residual = pl.pallas_call(
        functools.partial(rim_kernel, times, steps, lags),
        out_shape=(hbm(steps, 3, rows_lat, width), hbm(steps, 3, rows_lat, width)),
        out_specs=(pl.BlockSpec(memory_space=pl.ANY),) * 2,
        scratch_shapes=[
            vmem(known + 3, 1, rows, LANES),
            *working(1, fields, 1),
            vmem(2 * steps, 3, rows_lat, width),
            pltpu.SemaphoreType.DMA((2 * steps, 3)),
        ],
        name="rim_part",
    )(*kept(own, strips, part, part_residual, evens, *odds))
    return updated, residual


def solution(mesh):
    in_specs = (P("tm", None, "gy", "gx"), P(None, "gy", "gx"))
    out_specs = (P("tm", None, "gy", "gx"), P("tm", None, "gy", "gx"))
    return jax.shard_map(step, mesh=mesh, in_specs=in_specs, out_specs=out_specs, check_vma=False)
```

```python
import cmath
import functools
import math
import operator

import jax
import jax.numpy as jnp
from jax import lax
from jax.experimental import pallas as pl
from jax.experimental.pallas import tpu as pltpu
from jax.sharding import PartitionSpec as P


CHEB = 6
COURANT = 1.5
CORIOLIS_MEAN = 0.3
CORIOLIS_SLOPE = 0.4
CIRCULANT = 0.1
SPECTRUM_EDGE = 5.0
REACH = CHEB + 1
HALO = 8
LANES = 128
VMEM_KEPT = 2**20
SUBLANES = 8


def polynomials(total):
    factor = math.exp(math.log(CIRCULANT) / total)
    table = [[0.0] * (CHEB + 1) for _ in range(total)]
    for k in range(total):
        angle = 2.0 * math.pi * k / total
        shift = complex(1.0 - factor * math.cos(angle), factor * math.sin(angle))
        edge = 1j * SPECTRUM_EDGE
        sigma = shift / edge
        rho_old = 1.0 / sigma
        update = [1.0 / shift] + [0.0] * CHEB
        solved = list(update)
        for _ in range(CHEB):
            misfit = [-shift * solved[j] - (solved[j - 1] if j else -1.0) for j in range(CHEB + 1)]
            rho_new = 1.0 / (2.0 * sigma - rho_old)
            update = [rho_new * rho_old * a + 2.0 * rho_new / edge * b for a, b in zip(update, misfit)]
            solved = [a + b for a, b in zip(solved, update)]
            rho_old = rho_new
        for lag in range(total):
            turn = cmath.exp(1j * angle * lag) / total
            for j in range(CHEB + 1):
                table[lag][j] += (turn * solved[j]).real * COURANT**j
    return table


def pair_up(axis, odd):
    count = lax.axis_size(axis)
    first = range(1 if odd else 0, count, 2)
    return [pair for i in first for pair in ((i, (i + 1) % count), ((i + 1) % count, i))]


def with_steps(axis, pairs, by):
    times, count = lax.axis_size("tm"), lax.axis_size(axis)
    return [(t * count + a, (t + by) % times * count + b) for t in range(times) for a, b in pairs]


def rotated(tiles, by):
    lane = lax.broadcasted_iota(jnp.int32, (SUBLANES, LANES), 1)
    turned = [pltpu.roll(tile, by % LANES, 1) for tile in tiles]
    if len(tiles) == 1:
        return turned
    edge = lane == (0 if by > 0 else LANES - 1)
    return [jnp.where(edge, turned[(w - by) % len(tiles)], turned[w]) for w in range(len(tiles))]


def dlon(tiles):
    return [east - west for east, west in zip(rotated(tiles, -1), rotated(tiles, 1))]


def around(load, q, tiles):
    north = load(q - 1) if q else [pltpu.roll(tile, 1, 0) for tile in load(tiles - 1)]
    south = load(q + 1) if q < tiles - 1 else [pltpu.roll(tile, SUBLANES - 1, 0) for tile in load(0)]
    return north, south


def dlat(load, q, tiles):
    north, south = around(load, q, tiles)
    return [s - n for s, n in zip(south, north)]


def dealt(ref, f, q):
    tiles = ref.shape[-2] // SUBLANES
    return [ref[f, w, pl.ds(q, SUBLANES, stride=tiles), :] for w in range(ref.shape[1])]


def gather_columns(tiles, width):
    lane = lax.broadcasted_iota(jnp.int32, (SUBLANES, LANES), 1)
    packed = jnp.zeros((SUBLANES, LANES), jnp.float32)
    half = LANES // 2
    for f, tile in enumerate(tiles):
        head = pltpu.roll(tile[:, :LANES], half + REACH * f, 1)
        tail = pltpu.roll(tile[:, width - LANES :], REACH * (f + 1), 1)
        at = lane - REACH * f
        packed = jnp.where((at >= 0) & (at < REACH), tail, packed)
        packed = jnp.where((at >= half) & (at < half + REACH), head, packed)
    return packed


def edge_kernel(steps, traj, init, zs_even, zs_odd, sems):
    rows_lat = traj.shape[-2]
    gy_even = lax.axis_index("gy") % 2 == 0
    copies = []
    for side, (target, south) in enumerate(((zs_even, gy_even), (zs_odd, jnp.logical_not(gy_even)))):
        rows = pl.ds(pl.multiple_of(jnp.where(south, rows_lat - HALO, 0), SUBLANES), HALO)
        for l in range(steps + 1):
            source = traj.at[l, :, rows, :] if l < steps else init.at[:, rows, :]
            copies.append(pltpu.make_async_copy(source, target.at[pl.ds(3 * l, 3)], sems.at[side, l]))
    for copy in copies:
        copy.start()
    for copy in copies:
        copy.wait()


def split_kernel(fields, traj, init, own, packs):
    rows_lat, width = traj.shape[-2:]
    for f in range(fields + 3):
        own[f] = traj[f // 3, f % 3] if f < fields else init[f - fields]
    for rows in range(rows_lat // SUBLANES):
        at = pl.ds(rows * SUBLANES, SUBLANES)
        packs[at, :] = gather_columns([own.at[f, at] for f in range(fields + 3)], width)


def other_pack_kernel(fields, *refs):
    own, others, packs = refs[0], refs[1:-1], refs[-1]
    gy_even = lax.axis_index("gy") % 2 == 0
    packs[0] = own[...]
    for d in range(len(others) // 3):
        raw, xr_even, xr_odd = others[3 * d : 3 * d + 3]
        rows_lat, width = raw.shape[-2:]
        even = gather_columns([xr_even.at[f] for f in range(fields)], width)
        odd = gather_columns([xr_odd.at[f] for f in range(fields)], width)
        packs[d + 1, :HALO, :] = jnp.where(gy_even, odd, even)
        packs[d + 1, HALO + rows_lat :, :] = jnp.where(gy_even, even, odd)
        for rows in range(rows_lat // SUBLANES):
            at = pl.ds(rows * SUBLANES, SUBLANES)
            tiles = [raw.at[f // 3, f % 3, at] for f in range(fields)]
            packs[d + 1, pl.ds(HALO + rows * SUBLANES, SUBLANES), :] = gather_columns(tiles, width)


def pack_kernel(fields, packs, zr_even, zr_odd, ys):
    width = zr_even.shape[-1]
    gy_even = lax.axis_index("gy") % 2 == 0
    rows_lat = packs.shape[0]
    even = gather_columns([zr_even.at[f] for f in range(fields + 3)], width)
    odd = gather_columns([zr_odd.at[f] for f in range(fields + 3)], width)
    ys[:HALO, :] = jnp.where(gy_even, odd, even)
    ys[HALO : HALO + rows_lat, :] = packs[...]
    ys[HALO + rows_lat :, :] = jnp.where(gy_even, even, odd)


def place(ext, base, own, even, odd):
    rows_lat, width = own[0].shape
    gy_even = lax.axis_index("gy") % 2 == 0
    for f, field in enumerate(own):
        for w in range(width // LANES):
            lanes = pl.ds(w * LANES, LANES)
            ext[base + f, w, pl.ds(HALO, rows_lat), :] = field[:, lanes]
            ext[base + f, w, pl.ds(0, HALO), :] = jnp.where(gy_even, odd[f, :, lanes], even[f, :, lanes])
            ext[base + f, w, pl.ds(rows_lat + HALO, HALO), :] = jnp.where(gy_even, even[f, :, lanes], odd[f, :, lanes])


def within(first, count, by=0):
    lane = lax.broadcasted_iota(jnp.int32, (SUBLANES, LANES), 1)
    return (lane - first - by) % LANES < count


def place_strips(strips, ext, count):
    tiles = ext.shape[1]
    for rows in range(ext.shape[2] // SUBLANES):
        rows = pl.ds(rows * SUBLANES, SUBLANES)
        for f in range(count):
            head = pltpu.roll(ext[f, 0, rows, :], LANES // 2 + REACH, 1)
            strips[f, rows, :] = jnp.where(within(LANES // 2 + REACH, 2 * REACH), head, ext[f, tiles - 1, rows, :])


def place_rim(rim, base, strips, at, count, slot, pack_even, pack_odd):
    half = LANES // 2
    lane = lax.broadcasted_iota(jnp.int32, (SUBLANES, LANES), 1)
    gx_even = lax.axis_index("gx") % 2 == 0
    from_odd = (lane < half) == gx_even
    outside = within(0, REACH) | within(half, REACH)
    for rows in range(strips.shape[1] // SUBLANES):
        rows = pl.ds(rows * SUBLANES, SUBLANES)
        both = jnp.where(from_odd, pack_odd[rows, :], pack_even[rows, :])
        for f in range(count):
            value = pltpu.roll(both, half - REACH * (slot + f), 1)
            rim[base + f, 0, rows, :] = jnp.where(outside, value, strips[at + f, rows, :])


def coriolis(q, rows_lat):
    gy = lax.axis_index("gy")
    nlat = rows_lat * lax.axis_size("gy")
    tiles = (rows_lat + 2 * HALO) // SUBLANES
    row = lax.broadcasted_iota(jnp.int32, (SUBLANES, LANES), 0) * tiles + (q - HALO) + gy * rows_lat
    row = jnp.where(row < 0, row + nlat, jnp.where(row >= nlat, row - nlat, row))
    return CORIOLIS_MEAN + CORIOLIS_SLOPE * ((row.astype(jnp.float32) + 0.5) / nlat - 0.5)


def tendency(load, q, tiles, rotation):
    h, u, v = (load(c, q) for c in range(3))

    def product(at):
        return [b + a * b for a, b in zip(load(0, at), load(2, at))]

    flow = dlon([b + a * b for a, b in zip(h, u)])
    east = [dlon(field) for field in (h, u, v)]
    north = [dlat(functools.partial(load, c), q, tiles) for c in range(3)]
    drift = dlat(product, q, tiles)
    out = ([], [], [])
    for w in range(len(h)):
        out[0].append(h[w] + COURANT * (flow[w] + drift[w]))
        out[1].append(u[w] - rotation * v[w] + COURANT * (east[0][w] + u[w] * east[1][w] + v[w] * north[1][w]))
        out[2].append(v[w] + rotation * u[w] + COURANT * (north[0][w] + u[w] * east[2][w] + v[w] * north[2][w]))
    return out


def horner(rate, weights, state, turn, write):
    outputs, (tiles, across) = range(len(weights)), state.shape[3:5]

    def blend(n, j, c, q):
        terms = lambda t: (w[j] * rate(3 * i + c, q, t) for i, w in enumerate(weights[n]))
        return [functools.reduce(operator.add, terms(t)) for t in range(across)]

    for q in range(tiles):
        for n in outputs:
            for c in range(3):
                for t, value in enumerate(blend(n, CHEB, c, q)):
                    state[0, n, c, q, t] = value
    for j in range(CHEB - 1, -1, -1):
        now, later = ((CHEB - 1 - j) % 2, (CHEB - j) % 2)
        for q in range(tiles):
            for n in outputs:
                load = lambda c, at, n=n: [state[now, n, c, at, t] for t in range(across)]
                h, u, v = (load(c, q) for c in range(3))
                east_h, east_u = (dlon(h), dlon(u))
                north_h, north_v = (dlat(functools.partial(load, c), q, tiles) for c in (0, 2))
                add = [blend(n, j, c, q) for c in range(3)]
                new = (
                    [add[0][t] + (east_u[t] + north_v[t]) for t in range(across)],
                    [add[1][t] + (east_h[t] - turn[q] * v[t]) for t in range(across)],
                    [add[2][t] + (north_h[t] + turn[q] * u[t]) for t in range(across)],
                )
                for c in range(3):
                    if j:
                        for t in range(across):
                            state[later, n, c, q, t] = new[c][t]
                    else:
                        write(n, c, q, new[c])


def weights_of(lags, lag):
    return [w * CIRCULANT ** (-lag / len(lags)) for w in lags[lag % len(lags)]]


def put(scratch, f, q, values):
    tiles = scratch.shape[-2] // SUBLANES
    for w, value in enumerate(values):
        scratch[f, w, pl.ds(q, SUBLANES, stride=tiles), :] = value


def block_of(scratch, f, rows_lat):
    return jnp.concatenate([scratch[f, w, HALO : HALO + rows_lat] for w in range(scratch.shape[1])], axis=1)


def residuals(times, steps, ext, rates, rotation, write):
    fields, first = 3 * steps, 3 * steps * times
    tiles = rates.shape[1]
    me = lax.axis_index("tm")
    for d in range(times):
        scale = jnp.where(me < d, jnp.float32(CIRCULANT), jnp.float32(1.0))
        for l in range(steps):
            at = d * fields + 3 * l
            before = (at - 3) if l else ((d + 1) % times * fields + fields - 3)
            for q in range(tiles):
                out = tendency(lambda c, row: dealt(ext, at + c, row), q, tiles, rotation[q])
                for c in range(3):
                    prior = dealt(ext, before + c, q)
                    if l == 0:
                        prior = [jnp.where(me == d, a, b) for a, b in zip(dealt(ext, first + c, q), prior)]
                    values = [a - b for a, b in zip(out[c], prior)]
                    if d == 0:
                        write(l, c, q, values)
                    for t, value in enumerate(values):
                        rates[at + c, q, t] = scale * value if d else value


def weights_for(times, steps, lags):
    return [
        [weights_of(lags, d * steps + n - m) for d in range(times) for m in range(steps)] for n in range(steps)
    ]


def own_kernel(steps, own, zr_even, zr_odd, ext, strips, rates):
    fields = 3 * steps
    rows_lat = own.shape[-2]
    tiles, _ = rates.shape[1:3]
    place(ext, 0, [own.at[f] for f in range(fields + 3)], zr_even, zr_odd)
    place_strips(strips, ext, fields + 3)
    rotation = [coriolis(q, rows_lat) for q in range(tiles)]
    for l in range(steps):
        for q in range(tiles):
            out = tendency(lambda c, row: dealt(ext, 3 * l + c, row), q, tiles, rotation[q])
            for c in range(3):
                values = out[c]
                if l:
                    values = [a - b for a, b in zip(values, dealt(ext, 3 * (l - 1) + c, q))]
                for t, value in enumerate(values):
                    rates[3 * l + c, q, t] = value


def block_kernel(times, steps, lags, ext_own, rates_own, *refs):
    fields = 3 * steps
    others = refs[: 3 * (times - 1)]
    strips, part, residual, ext, rates, state, scratch = refs[3 * (times - 1) :]
    rows_lat = ext.shape[2] - 2 * HALO
    tiles = rates.shape[1]
    for d in range(1, times):
        raw, xr_even, xr_odd = others[3 * (d - 1) : 3 * d]
        blocks = [raw.at[f // 3, f % 3] for f in range(fields)]
        place(ext, (d - 1) * fields, blocks, xr_even, xr_odd)
    rotation = [coriolis(q, rows_lat) for q in range(tiles)]
    me = lax.axis_index("tm")

    def before(d, c, q):
        last = dealt(ext_own, fields - 3 + c, q) if d + 1 == times else dealt(ext, (d + 1) * fields - 3 + c, q)
        return [jnp.where(me == d, a, b) for a, b in zip(dealt(ext_own, fields + c, q), last)]

    for q in range(tiles):
        for f in range(fields):
            values = [rates_own[f, q, t] for t in range(rates.shape[2])]
            if f < 3:
                values = [a - b for a, b in zip(values, before(0, f, q))]
                for t, value in enumerate(values):
                    rates[f, q, t] = value
            put(scratch, f, q, values)
    for d in range(1, times):
        scale = jnp.where(me < d, jnp.float32(CIRCULANT), jnp.float32(1.0))
        for l in range(steps):
            at = (d - 1) * fields + 3 * l
            for q in range(tiles):
                out = tendency(lambda c, row: dealt(ext, at + c, row), q, tiles, rotation[q])
                for c in range(3):
                    prior = dealt(ext, at - 3 + c, q) if l else before(d, c, q)
                    for t, value in enumerate(out[c]):
                        rates[3 + at + c, q, t] = scale * (value - prior[t])
    for l in range(steps):
        for c in range(3):
            residual[l, c] = block_of(scratch, 3 * l + c, rows_lat)
    place_strips(strips, ext, (times - 1) * fields)
    turn = [r * (1.0 / COURANT) for r in rotation]
    weights = weights_for(times, steps, lags)

    def rate(k, q, t):
        return rates[k, q, t] if k < 3 else rates_own[k, q, t] if k < fields else rates[k - fields + 3, q, t]

    horner(rate, weights, state, turn, lambda n, c, q, values: put(scratch, fields + 3 * n + c, q, values))
    for n in range(steps):
        for c in range(3):
            part[n, c] = block_of(scratch, fields + 3 * n + c, rows_lat)


APART = 4 * REACH


def rim_kernel(times, steps, lags, own, strips_own, strips, part, part_residual, yr_even, yr_odd, *refs):
    fields, half = 3 * steps, LANES // 2
    updated, residual, rim, rates, state, scratch, ready, sems = refs[times - 1 :]
    rows_lat, width = own.shape[-2:]
    tiles = rates.shape[1]
    place_rim(rim, 0, strips_own, 0, fields, 0, yr_even.at[0], yr_odd)
    place_rim(rim, times * fields, strips_own, fields, 3, fields, yr_even.at[0], yr_odd)
    for d in range(1, times):
        place_rim(rim, d * fields, strips, (d - 1) * fields, fields, 0, yr_even.at[d], refs[d - 1])
    rotation = [coriolis(q, rows_lat) for q in range(tiles)]
    residuals(times, steps, rim, rates, rotation, lambda l, c, q, values: put(scratch, 3 * l + c, q, values))
    lane = lax.broadcasted_iota(jnp.int32, (rows_lat, LANES), 1)

    def merged(value, strip, by):
        tail = pltpu.roll(strip, LANES - by, 1) if by else strip
        head = pltpu.roll(strip, half - REACH - by, 1)
        value = [value[:, w * LANES : (w + 1) * LANES] for w in range(width // LANES)]
        value[0] = jnp.where(lane < REACH, head, value[0])
        value[-1] = jnp.where(lane >= LANES - REACH, tail, value[-1])
        return jnp.concatenate(value, axis=1)

    copies = []
    for l in range(steps):
        for c in range(3):
            ready[l, c] = merged(part_residual[l, c], block_of(scratch, 3 * l + c, rows_lat), 0)
            copies.append(pltpu.make_async_copy(ready.at[l, c], residual.at[l, c], sems.at[l, c]))
            copies[-1].start()

    second = within(LANES - 2 * REACH, 3 * REACH, APART) | within(half, 3 * REACH, APART)
    for f in range(times * fields):
        for q in range(tiles):
            rates[f, q, 0] = jnp.where(second, pltpu.roll(rates[f, q, 0], APART, 1), rates[f, q, 0])
    turn = [r * (1.0 / COURANT) for r in rotation]
    plain = weights_for(times, steps, lags)
    for n in range(0, steps, 2):
        pair = [
            [[jnp.where(second, b, a) for a, b in zip(*both)] for both in zip(plain[n], plain[min(n + 1, steps - 1)])]
        ]
        horner(lambda k, q, t: rates[k, q, t], pair, state, turn, lambda _, c, q, values: put(scratch, c, q, values))
        for c in range(3):
            strip = block_of(scratch, c, rows_lat)
            for m in range(n, min(n + 2, steps)):
                ready[steps + m, c] = own[3 * m + c] - merged(part[m, c], strip, (m - n) * APART)
                copies.append(pltpu.make_async_copy(ready.at[steps + m, c], updated.at[m, c], sems.at[steps + m, c]))
                copies[-1].start()
    for copy in copies:
        copy.wait()


def step(trajectory, initial):
    steps, _, rows_lat, width = trajectory.shape
    times = lax.axis_size("tm")
    fields = 3 * steps
    lags = polynomials(times * steps)

    def vmem(*shape):
        return pltpu.VMEM(shape, jnp.float32)

    rows, across = (rows_lat + 2 * HALO, width // LANES)
    known = times * fields

    def hbm(*shape):
        return jax.ShapeDtypeStruct(shape, jnp.float32)

    fits = 4 * known * rows * width <= VMEM_KEPT
    near = vmem if fits else hbm

    def kept(*arrays):
        return [pltpu.with_memory_space_constraint(array, pltpu.VMEM) if fits else array for array in arrays]

    zs_even, zs_odd = pl.pallas_call(
        functools.partial(edge_kernel, steps),
        in_specs=[pl.BlockSpec(memory_space=pl.ANY)] * 2,
        out_shape=(near(fields + 3, HALO, width), near(fields + 3, HALO, width)),
        scratch_shapes=[pltpu.SemaphoreType.DMA((2, steps + 1))],
        name="edge_rows",
    )(trajectory, initial)
    zr_odd = lax.ppermute(zs_odd, "gy", pair_up("gy", True))
    zr_even = lax.ppermute(zs_even, "gy", pair_up("gy", False))
    own, packs = pl.pallas_call(
        functools.partial(split_kernel, fields),
        out_shape=(near(fields + 3, rows_lat, width), near(rows_lat, LANES)),
        name="split_block",
    )(trajectory, initial)
    shifts = [[(t, (t + d) % times) for t in range(times)] for d in range(times)]
    raws = [lax.ppermute(trajectory, "tm", shifts[d]) for d in range(1, times)]

    ys = pl.pallas_call(
        functools.partial(pack_kernel, fields),
        out_shape=near(rows, LANES),
        name="pack_edges",
    )(*kept(packs, zr_even, zr_odd))

    even, odd = (pair_up("gx", False), pair_up("gx", True))
    xr_even = [lax.ppermute(zr_even[:fields], "tm", shifts[d]) for d in range(1, times)]
    xr_odd = [lax.ppermute(zr_odd[:fields], "tm", shifts[d]) for d in range(1, times)]
    odds = [lax.ppermute(ys, ("tm", "gx"), with_steps("gx", odd, d)) for d in range(1, times)]
    odds.insert(0, lax.ppermute(ys, "gx", odd))
    known_of = [each for both in zip(raws, xr_even, xr_odd) for each in both]
    ys_all = pl.pallas_call(
        functools.partial(other_pack_kernel, fields),
        out_shape=near(times, rows, LANES),
        name="pack_others",
    )(*kept(ys, *known_of))
    evens = lax.ppermute(ys_all, "gx", even)

    dealt_out = (rows // SUBLANES, across, SUBLANES, LANES)
    ext_own, strips_own, rates_own = pl.pallas_call(
        functools.partial(own_kernel, steps),
        out_shape=(
            near(fields + 3, across, rows, LANES),
            near(fields + 3, rows, LANES),
            near(fields, *dealt_out),
        ),
        name="own_part",
    )(*kept(own, zr_even, zr_odd))
    strips, part, part_residual = pl.pallas_call(
        functools.partial(block_kernel, times, steps, lags),
        out_shape=(near(known - fields, rows, LANES), near(steps, 3, rows_lat, width), near(steps, 3, rows_lat, width)),
        scratch_shapes=[
            vmem(known - fields, across, rows, LANES),
            vmem(known - fields + 3, *dealt_out),
            vmem(2, steps, 3, *dealt_out),
            vmem(2 * fields, across, rows, LANES),
        ],
        name="block_part",
    )(*kept(ext_own, rates_own, *known_of))
    updated, residual = pl.pallas_call(
        functools.partial(rim_kernel, times, steps, lags),
        out_shape=(hbm(steps, 3, rows_lat, width), hbm(steps, 3, rows_lat, width)),
        out_specs=(pl.BlockSpec(memory_space=pl.ANY),) * 2,
        scratch_shapes=[
            vmem(known + 3, 1, rows, LANES),
            vmem(known, rows // SUBLANES, 1, SUBLANES, LANES),
            vmem(2, 1, 3, rows // SUBLANES, 1, SUBLANES, LANES),
            vmem(fields, 1, rows, LANES),
            vmem(2 * steps, 3, rows_lat, width),
            pltpu.SemaphoreType.DMA((2 * steps, 3)),
        ],
        name="rim_part",
    )(*kept(own, strips_own, strips, part, part_residual, evens, *odds))
    return updated, residual


def solution(mesh):
    in_specs = (P("tm", None, "gy", "gx"), P(None, "gy", "gx"))
    out_specs = (P("tm", None, "gy", "gx"), P("tm", None, "gy", "gx"))
    return jax.shard_map(step, mesh=mesh, in_specs=in_specs, out_specs=out_specs, check_vma=False)
```

```python
import cmath
import functools
import math
import operator

import jax
import jax.numpy as jnp
from jax import lax
from jax.experimental import pallas as pl
from jax.experimental.pallas import tpu as pltpu
from jax.sharding import PartitionSpec as P


CHEB = 6
COURANT = 1.5
CORIOLIS_MEAN = 0.3
CORIOLIS_SLOPE = 0.4
CIRCULANT = 0.1
SPECTRUM_EDGE = 5.0
REACH = CHEB + 1
HALO = 8
LANES = 128
VMEM_KEPT = 2**20
SUBLANES = 8


def polynomials(total):
    factor = math.exp(math.log(CIRCULANT) / total)
    table = [[0.0] * (CHEB + 1) for _ in range(total)]
    for k in range(total):
        angle = 2.0 * math.pi * k / total
        shift = complex(1.0 - factor * math.cos(angle), factor * math.sin(angle))
        edge = 1j * SPECTRUM_EDGE
        sigma = shift / edge
        rho_old = 1.0 / sigma
        update = [1.0 / shift] + [0.0] * CHEB
        solved = list(update)
        for _ in range(CHEB):
            misfit = [-shift * solved[j] - (solved[j - 1] if j else -1.0) for j in range(CHEB + 1)]
            rho_new = 1.0 / (2.0 * sigma - rho_old)
            update = [rho_new * rho_old * a + 2.0 * rho_new / edge * b for a, b in zip(update, misfit)]
            solved = [a + b for a, b in zip(solved, update)]
            rho_old = rho_new
        for lag in range(total):
            turn = cmath.exp(1j * angle * lag) / total
            for j in range(CHEB + 1):
                table[lag][j] += (turn * solved[j]).real * COURANT**j
    return table


def pair_up(axis, odd):
    count = lax.axis_size(axis)
    first = range(1 if odd else 0, count, 2)
    return [pair for i in first for pair in ((i, (i + 1) % count), ((i + 1) % count, i))]


def with_steps(axis, pairs, by):
    times, count = lax.axis_size("tm"), lax.axis_size(axis)
    return [(t * count + a, (t + by) % times * count + b) for t in range(times) for a, b in pairs]


def rotated(tiles, by):
    lane = lax.broadcasted_iota(jnp.int32, (SUBLANES, LANES), 1)
    turned = [pltpu.roll(tile, by % LANES, 1) for tile in tiles]
    if len(tiles) == 1:
        return turned
    edge = lane == (0 if by > 0 else LANES - 1)
    return [jnp.where(edge, turned[(w - by) % len(tiles)], turned[w]) for w in range(len(tiles))]


def dlon(tiles):
    return [east - west for east, west in zip(rotated(tiles, -1), rotated(tiles, 1))]


def around(load, q, tiles):
    north = load(q - 1) if q else [pltpu.roll(tile, 1, 0) for tile in load(tiles - 1)]
    south = load(q + 1) if q < tiles - 1 else [pltpu.roll(tile, SUBLANES - 1, 0) for tile in load(0)]
    return north, south


def dlat(load, q, tiles):
    north, south = around(load, q, tiles)
    return [s - n for s, n in zip(south, north)]


def dealt(ref, f, q):
    tiles = ref.shape[-2] // SUBLANES
    return [ref[f, w, pl.ds(q, SUBLANES, stride=tiles), :] for w in range(ref.shape[1])]


def gather_columns(tiles, width):
    lane = lax.broadcasted_iota(jnp.int32, (SUBLANES, LANES), 1)
    packed = jnp.zeros((SUBLANES, LANES), jnp.float32)
    half = LANES // 2
    for f, tile in enumerate(tiles):
        head = pltpu.roll(tile[:, :LANES], half + REACH * f, 1)
        tail = pltpu.roll(tile[:, width - LANES :], REACH * (f + 1), 1)
        at = lane - REACH * f
        packed = jnp.where((at >= 0) & (at < REACH), tail, packed)
        packed = jnp.where((at >= half) & (at < half + REACH), head, packed)
    return packed


def edge_kernel(steps, traj, init, zs_even, zs_odd, sems):
    rows_lat = traj.shape[-2]
    copies = []
    for side, (target, south) in enumerate(((zs_even, False), (zs_odd, True))):
        rows = pl.ds(rows_lat - HALO if south else 0, HALO)
        for l in range(steps + 1):
            source = traj.at[l, :, rows, :] if l < steps else init.at[:, rows, :]
            copies.append(pltpu.make_async_copy(source, target.at[pl.ds(3 * l, 3)], sems.at[side, l]))
    for copy in copies:
        copy.start()
    for copy in copies:
        copy.wait()


def split_kernel(fields, traj, init, own, packs):
    rows_lat, width = traj.shape[-2:]
    for f in range(fields + 3):
        own[f] = traj[f // 3, f % 3] if f < fields else init[f - fields]
    for rows in range(rows_lat // SUBLANES):
        at = pl.ds(rows * SUBLANES, SUBLANES)
        packs[at, :] = gather_columns([own.at[f, at] for f in range(fields + 3)], width)


def other_pack_kernel(fields, *refs):
    own, others, packs = refs[0], refs[1:-1], refs[-1]
    packs[0] = own[...]
    for d in range(len(others) // 3):
        raw, xr_even, xr_odd = others[3 * d : 3 * d + 3]
        rows_lat, width = raw.shape[-2:]
        even = gather_columns([xr_even.at[f] for f in range(fields)], width)
        odd = gather_columns([xr_odd.at[f] for f in range(fields)], width)
        packs[d + 1, :HALO, :] = odd
        packs[d + 1, HALO + rows_lat :, :] = even
        for rows in range(rows_lat // SUBLANES):
            at = pl.ds(rows * SUBLANES, SUBLANES)
            tiles = [raw.at[f // 3, f % 3, at] for f in range(fields)]
            packs[d + 1, pl.ds(HALO + rows * SUBLANES, SUBLANES), :] = gather_columns(tiles, width)


def pack_kernel(fields, packs, zr_even, zr_odd, ys):
    width = zr_even.shape[-1]
    rows_lat = packs.shape[0]
    even = gather_columns([zr_even.at[f] for f in range(fields + 3)], width)
    odd = gather_columns([zr_odd.at[f] for f in range(fields + 3)], width)
    ys[:HALO, :] = odd
    ys[HALO : HALO + rows_lat, :] = packs[...]
    ys[HALO + rows_lat :, :] = even


def place(ext, base, own, even, odd):
    rows_lat, width = own[0].shape
    for f, field in enumerate(own):
        for w in range(width // LANES):
            lanes = pl.ds(w * LANES, LANES)
            ext[base + f, w, pl.ds(HALO, rows_lat), :] = field[:, lanes]
            ext[base + f, w, pl.ds(0, HALO), :] = odd[f, :, lanes]
            ext[base + f, w, pl.ds(rows_lat + HALO, HALO), :] = even[f, :, lanes]


def within(first, count, by=0):
    lane = lax.broadcasted_iota(jnp.int32, (SUBLANES, LANES), 1)
    return (lane - first - by) % LANES < count


def place_strips(strips, ext, count):
    tiles = ext.shape[1]
    for rows in range(ext.shape[2] // SUBLANES):
        rows = pl.ds(rows * SUBLANES, SUBLANES)
        for f in range(count):
            head = pltpu.roll(ext[f, 0, rows, :], LANES // 2 + REACH, 1)
            strips[f, rows, :] = jnp.where(within(LANES // 2 + REACH, 2 * REACH), head, ext[f, tiles - 1, rows, :])


def place_rim(rim, base, strips, at, count, slot, pack_even, pack_odd):
    half = LANES // 2
    lane = lax.broadcasted_iota(jnp.int32, (SUBLANES, LANES), 1)
    gx_even = lax.axis_index("gx") % 2 == 0
    from_odd = (lane < half) == gx_even
    outside = within(0, REACH) | within(half, REACH)
    for rows in range(strips.shape[1] // SUBLANES):
        rows = pl.ds(rows * SUBLANES, SUBLANES)
        both = jnp.where(from_odd, pack_odd[rows, :], pack_even[rows, :])
        for f in range(count):
            value = pltpu.roll(both, half - REACH * (slot + f), 1)
            rim[base + f, 0, rows, :] = jnp.where(outside, value, strips[at + f, rows, :])


def coriolis(q, rows_lat):
    gy = lax.axis_index("gy")
    nlat = rows_lat * lax.axis_size("gy")
    tiles = (rows_lat + 2 * HALO) // SUBLANES
    row = lax.broadcasted_iota(jnp.int32, (SUBLANES, LANES), 0) * tiles + (q - HALO) + gy * rows_lat
    row = jnp.where(row < 0, row + nlat, jnp.where(row >= nlat, row - nlat, row))
    return CORIOLIS_MEAN + CORIOLIS_SLOPE * ((row.astype(jnp.float32) + 0.5) / nlat - 0.5)


def tendency(load, q, tiles, rotation):
    h, u, v = (load(c, q) for c in range(3))

    def product(at):
        return [b + a * b for a, b in zip(load(0, at), load(2, at))]

    flow = dlon([b + a * b for a, b in zip(h, u)])
    east = [dlon(field) for field in (h, u, v)]
    north = [dlat(functools.partial(load, c), q, tiles) for c in range(3)]
    drift = dlat(product, q, tiles)
    out = ([], [], [])
    for w in range(len(h)):
        out[0].append(h[w] + COURANT * (flow[w] + drift[w]))
        out[1].append(u[w] - rotation * v[w] + COURANT * (east[0][w] + u[w] * east[1][w] + v[w] * north[1][w]))
        out[2].append(v[w] + rotation * u[w] + COURANT * (north[0][w] + u[w] * east[2][w] + v[w] * north[2][w]))
    return out


def horner(rate, weights, state, turn, write):
    outputs, (tiles, across) = range(len(weights)), state.shape[3:5]

    def blend(n, j, c, q):
        terms = lambda t: (w[j] * rate(3 * i + c, q, t) for i, w in enumerate(weights[n]))
        return [functools.reduce(operator.add, terms(t)) for t in range(across)]

    for q in range(tiles):
        for n in outputs:
            for c in range(3):
                for t, value in enumerate(blend(n, CHEB, c, q)):
                    state[0, n, c, q, t] = value
    for j in range(CHEB - 1, -1, -1):
        now, later = ((CHEB - 1 - j) % 2, (CHEB - j) % 2)
        for q in range(tiles):
            for n in outputs:
                load = lambda c, at, n=n: [state[now, n, c, at, t] for t in range(across)]
                h, u, v = (load(c, q) for c in range(3))
                east_h, east_u = (dlon(h), dlon(u))
                north_h, north_v = (dlat(functools.partial(load, c), q, tiles) for c in (0, 2))
                add = [blend(n, j, c, q) for c in range(3)]
                new = (
                    [add[0][t] + (east_u[t] + north_v[t]) for t in range(across)],
                    [add[1][t] + (east_h[t] - turn[q] * v[t]) for t in range(across)],
                    [add[2][t] + (north_h[t] + turn[q] * u[t]) for t in range(across)],
                )
                for c in range(3):
                    if j:
                        for t in range(across):
                            state[later, n, c, q, t] = new[c][t]
                    else:
                        write(n, c, q, new[c])


def weights_of(lags, lag):
    return [w * CIRCULANT ** (-lag / len(lags)) for w in lags[lag % len(lags)]]


def put(scratch, f, q, values):
    tiles = scratch.shape[-2] // SUBLANES
    for w, value in enumerate(values):
        scratch[f, w, pl.ds(q, SUBLANES, stride=tiles), :] = value


def block_of(scratch, f, rows_lat):
    return jnp.concatenate([scratch[f, w, HALO : HALO + rows_lat] for w in range(scratch.shape[1])], axis=1)


def residuals(times, steps, ext, rates, rotation, write):
    fields, first = 3 * steps, 3 * steps * times
    tiles = rates.shape[1]
    me = lax.axis_index("tm")
    for d in range(times):
        scale = jnp.where(me < d, jnp.float32(CIRCULANT), jnp.float32(1.0))
        for l in range(steps):
            at = d * fields + 3 * l
            before = (at - 3) if l else ((d + 1) % times * fields + fields - 3)
            for q in range(tiles):
                out = tendency(lambda c, row: dealt(ext, at + c, row), q, tiles, rotation[q])
                for c in range(3):
                    prior = dealt(ext, before + c, q)
                    if l == 0:
                        prior = [jnp.where(me == d, a, b) for a, b in zip(dealt(ext, first + c, q), prior)]
                    values = [a - b for a, b in zip(out[c], prior)]
                    if d == 0:
                        write(l, c, q, values)
                    for t, value in enumerate(values):
                        rates[at + c, q, t] = scale * value if d else value


def weights_for(times, steps, lags):
    return [
        [weights_of(lags, d * steps + n - m) for d in range(times) for m in range(steps)] for n in range(steps)
    ]


def own_kernel(steps, own, zr_even, zr_odd, ext, strips, rates):
    fields = 3 * steps
    rows_lat = own.shape[-2]
    tiles, _ = rates.shape[1:3]
    place(ext, 0, [own.at[f] for f in range(fields + 3)], zr_even, zr_odd)
    place_strips(strips, ext, fields + 3)
    rotation = [coriolis(q, rows_lat) for q in range(tiles)]
    for l in range(steps):
        for q in range(tiles):
            out = tendency(lambda c, row: dealt(ext, 3 * l + c, row), q, tiles, rotation[q])
            for c in range(3):
                values = out[c]
                if l:
                    values = [a - b for a, b in zip(values, dealt(ext, 3 * (l - 1) + c, q))]
                for t, value in enumerate(values):
                    rates[3 * l + c, q, t] = value


def block_kernel(times, steps, lags, ext_own, rates_own, *refs):
    fields = 3 * steps
    others = refs[: 3 * (times - 1)]
    strips, part, residual, ext, rates, state, scratch = refs[3 * (times - 1) :]
    rows_lat = ext.shape[2] - 2 * HALO
    tiles = rates.shape[1]
    for d in range(1, times):
        raw, xr_even, xr_odd = others[3 * (d - 1) : 3 * d]
        blocks = [raw.at[f // 3, f % 3] for f in range(fields)]
        place(ext, (d - 1) * fields, blocks, xr_even, xr_odd)
    rotation = [coriolis(q, rows_lat) for q in range(tiles)]
    me = lax.axis_index("tm")

    def before(d, c, q):
        last = dealt(ext_own, fields - 3 + c, q) if d + 1 == times else dealt(ext, (d + 1) * fields - 3 + c, q)
        return [jnp.where(me == d, a, b) for a, b in zip(dealt(ext_own, fields + c, q), last)]

    for q in range(tiles):
        for f in range(fields):
            values = [rates_own[f, q, t] for t in range(rates.shape[2])]
            if f < 3:
                values = [a - b for a, b in zip(values, before(0, f, q))]
                for t, value in enumerate(values):
                    rates[f, q, t] = value
            put(scratch, f, q, values)
    for d in range(1, times):
        scale = jnp.where(me < d, jnp.float32(CIRCULANT), jnp.float32(1.0))
        for l in range(steps):
            at = (d - 1) * fields + 3 * l
            for q in range(tiles):
                out = tendency(lambda c, row: dealt(ext, at + c, row), q, tiles, rotation[q])
                for c in range(3):
                    prior = dealt(ext, at - 3 + c, q) if l else before(d, c, q)
                    for t, value in enumerate(out[c]):
                        rates[3 + at + c, q, t] = scale * (value - prior[t])
    for l in range(steps):
        for c in range(3):
            residual[l, c] = block_of(scratch, 3 * l + c, rows_lat)
    place_strips(strips, ext, (times - 1) * fields)
    turn = [r * (1.0 / COURANT) for r in rotation]
    weights = weights_for(times, steps, lags)

    def rate(k, q, t):
        return rates[k, q, t] if k < 3 else rates_own[k, q, t] if k < fields else rates[k - fields + 3, q, t]

    horner(rate, weights, state, turn, lambda n, c, q, values: put(scratch, fields + 3 * n + c, q, values))
    for n in range(steps):
        for c in range(3):
            part[n, c] = block_of(scratch, fields + 3 * n + c, rows_lat)


APART = 4 * REACH


def rim_kernel(times, steps, lags, own, strips_own, strips, part, part_residual, yr_even, yr_odd, *refs):
    fields, half = 3 * steps, LANES // 2
    updated, residual, rim, rates, state, scratch, ready, sems = refs[times - 1 :]
    rows_lat, width = own.shape[-2:]
    tiles = rates.shape[1]
    place_rim(rim, 0, strips_own, 0, fields, 0, yr_even.at[0], yr_odd)
    place_rim(rim, times * fields, strips_own, fields, 3, fields, yr_even.at[0], yr_odd)
    for d in range(1, times):
        place_rim(rim, d * fields, strips, (d - 1) * fields, fields, 0, yr_even.at[d], refs[d - 1])
    rotation = [coriolis(q, rows_lat) for q in range(tiles)]
    residuals(times, steps, rim, rates, rotation, lambda l, c, q, values: put(scratch, 3 * l + c, q, values))
    lane = lax.broadcasted_iota(jnp.int32, (rows_lat, LANES), 1)

    def merged(value, strip, by):
        tail = pltpu.roll(strip, LANES - by, 1) if by else strip
        head = pltpu.roll(strip, half - REACH - by, 1)
        value = [value[:, w * LANES : (w + 1) * LANES] for w in range(width // LANES)]
        value[0] = jnp.where(lane < REACH, head, value[0])
        value[-1] = jnp.where(lane >= LANES - REACH, tail, value[-1])
        return jnp.concatenate(value, axis=1)

    copies = []
    for l in range(steps):
        for c in range(3):
            ready[l, c] = merged(part_residual[l, c], block_of(scratch, 3 * l + c, rows_lat), 0)
            copies.append(pltpu.make_async_copy(ready.at[l, c], residual.at[l, c], sems.at[l, c]))
            copies[-1].start()

    second = within(LANES - 2 * REACH, 3 * REACH, APART) | within(half, 3 * REACH, APART)
    for f in range(times * fields):
        for q in range(tiles):
            rates[f, q, 0] = jnp.where(second, pltpu.roll(rates[f, q, 0], APART, 1), rates[f, q, 0])
    turn = [r * (1.0 / COURANT) for r in rotation]
    plain = weights_for(times, steps, lags)
    for n in range(0, steps, 2):
        pair = [
            [[jnp.where(second, b, a) for a, b in zip(*both)] for both in zip(plain[n], plain[min(n + 1, steps - 1)])]
        ]
        horner(lambda k, q, t: rates[k, q, t], pair, state, turn, lambda _, c, q, values: put(scratch, c, q, values))
        for c in range(3):
            strip = block_of(scratch, c, rows_lat)
            for m in range(n, min(n + 2, steps)):
                ready[steps + m, c] = own[3 * m + c] - merged(part[m, c], strip, (m - n) * APART)
                copies.append(pltpu.make_async_copy(ready.at[steps + m, c], updated.at[m, c], sems.at[steps + m, c]))
                copies[-1].start()
    for copy in copies:
        copy.wait()


def step(trajectory, initial):
    steps, _, rows_lat, width = trajectory.shape
    times = lax.axis_size("tm")
    fields = 3 * steps
    lags = polynomials(times * steps)

    def vmem(*shape):
        return pltpu.VMEM(shape, jnp.float32)

    rows, across = (rows_lat + 2 * HALO, width // LANES)
    known = times * fields

    def hbm(*shape):
        return jax.ShapeDtypeStruct(shape, jnp.float32)

    fits = 4 * known * rows * width <= VMEM_KEPT
    near = vmem if fits else hbm

    def kept(*arrays):
        return [pltpu.with_memory_space_constraint(array, pltpu.VMEM) if fits else array for array in arrays]

    zs_even, zs_odd = pl.pallas_call(
        functools.partial(edge_kernel, steps),
        in_specs=[pl.BlockSpec(memory_space=pl.ANY)] * 2,
        out_shape=(near(fields + 3, HALO, width), near(fields + 3, HALO, width)),
        scratch_shapes=[pltpu.SemaphoreType.DMA((2, steps + 1))],
        name="edge_rows",
    )(trajectory, initial)
    count = lax.axis_size("gy")
    zr_odd = lax.ppermute(zs_odd, "gy", [(i, (i + 1) % count) for i in range(count)])
    zr_even = lax.ppermute(zs_even, "gy", [((i + 1) % count, i) for i in range(count)])
    own, packs = pl.pallas_call(
        functools.partial(split_kernel, fields),
        out_shape=(near(fields + 3, rows_lat, width), near(rows_lat, LANES)),
        name="split_block",
    )(trajectory, initial)
    shifts = [[(t, (t + d) % times) for t in range(times)] for d in range(times)]
    raws = [lax.ppermute(trajectory, "tm", shifts[d]) for d in range(1, times)]

    ys = pl.pallas_call(
        functools.partial(pack_kernel, fields),
        out_shape=near(rows, LANES),
        name="pack_edges",
    )(*kept(packs, zr_even, zr_odd))

    even, odd = (pair_up("gx", False), pair_up("gx", True))
    xr_even = [lax.ppermute(zr_even[:fields], "tm", shifts[d]) for d in range(1, times)]
    xr_odd = [lax.ppermute(zr_odd[:fields], "tm", shifts[d]) for d in range(1, times)]
    odds = [lax.ppermute(ys, ("tm", "gx"), with_steps("gx", odd, d)) for d in range(1, times)]
    odds.insert(0, lax.ppermute(ys, "gx", odd))
    known_of = [each for both in zip(raws, xr_even, xr_odd) for each in both]
    ys_all = pl.pallas_call(
        functools.partial(other_pack_kernel, fields),
        out_shape=near(times, rows, LANES),
        name="pack_others",
    )(*kept(ys, *known_of))
    evens = lax.ppermute(ys_all, "gx", even)

    dealt_out = (rows // SUBLANES, across, SUBLANES, LANES)
    ext_own, strips_own, rates_own = pl.pallas_call(
        functools.partial(own_kernel, steps),
        out_shape=(
            near(fields + 3, across, rows, LANES),
            near(fields + 3, rows, LANES),
            near(fields, *dealt_out),
        ),
        name="own_part",
    )(*kept(own, zr_even, zr_odd))
    strips, part, part_residual = pl.pallas_call(
        functools.partial(block_kernel, times, steps, lags),
        out_shape=(near(known - fields, rows, LANES), near(steps, 3, rows_lat, width), near(steps, 3, rows_lat, width)),
        scratch_shapes=[
            vmem(known - fields, across, rows, LANES),
            vmem(known - fields + 3, *dealt_out),
            vmem(2, steps, 3, *dealt_out),
            vmem(2 * fields, across, rows, LANES),
        ],
        name="block_part",
    )(*kept(ext_own, rates_own, *known_of))
    updated, residual = pl.pallas_call(
        functools.partial(rim_kernel, times, steps, lags),
        out_shape=(hbm(steps, 3, rows_lat, width), hbm(steps, 3, rows_lat, width)),
        out_specs=(pl.BlockSpec(memory_space=pl.ANY),) * 2,
        scratch_shapes=[
            vmem(known + 3, 1, rows, LANES),
            vmem(known, rows // SUBLANES, 1, SUBLANES, LANES),
            vmem(2, 1, 3, rows // SUBLANES, 1, SUBLANES, LANES),
            vmem(fields, 1, rows, LANES),
            vmem(2 * steps, 3, rows_lat, width),
            pltpu.SemaphoreType.DMA((2 * steps, 3)),
        ],
        name="rim_part",
    )(*kept(own, strips_own, strips, part, part_residual, evens, *odds))
    return updated, residual


def solution(mesh):
    in_specs = (P("tm", None, "gy", "gx"), P(None, "gy", "gx"))
    out_specs = (P("tm", None, "gy", "gx"), P("tm", None, "gy", "gx"))
    return jax.shard_map(step, mesh=mesh, in_specs=in_specs, out_specs=out_specs, check_vma=False)
```

```python
import cmath
import functools
import math
import operator

import jax
import jax.numpy as jnp
from jax import lax
from jax.experimental import pallas as pl
from jax.experimental.pallas import tpu as pltpu
from jax.sharding import PartitionSpec as P


CHEB = 6
COURANT = 1.5
CORIOLIS_MEAN = 0.3
CORIOLIS_SLOPE = 0.4
CIRCULANT = 0.1
SPECTRUM_EDGE = 5.0
REACH = CHEB + 1
HALO = 8
LANES = 128
VMEM_KEPT = 2**20
SUBLANES = 8


def polynomials(total):
    factor = math.exp(math.log(CIRCULANT) / total)
    table = [[0.0] * (CHEB + 1) for _ in range(total)]
    for k in range(total):
        angle = 2.0 * math.pi * k / total
        shift = complex(1.0 - factor * math.cos(angle), factor * math.sin(angle))
        edge = 1j * SPECTRUM_EDGE
        sigma = shift / edge
        rho_old = 1.0 / sigma
        update = [1.0 / shift] + [0.0] * CHEB
        solved = list(update)
        for _ in range(CHEB):
            misfit = [-shift * solved[j] - (solved[j - 1] if j else -1.0) for j in range(CHEB + 1)]
            rho_new = 1.0 / (2.0 * sigma - rho_old)
            update = [rho_new * rho_old * a + 2.0 * rho_new / edge * b for a, b in zip(update, misfit)]
            solved = [a + b for a, b in zip(solved, update)]
            rho_old = rho_new
        for lag in range(total):
            turn = cmath.exp(1j * angle * lag) / total
            for j in range(CHEB + 1):
                table[lag][j] += (turn * solved[j]).real * COURANT**j
    return table


def pair_up(axis, odd):
    count = lax.axis_size(axis)
    first = range(1 if odd else 0, count, 2)
    return [pair for i in first for pair in ((i, (i + 1) % count), ((i + 1) % count, i))]


def with_steps(axis, pairs, by):
    times, count = lax.axis_size("tm"), lax.axis_size(axis)
    return [(t * count + a, (t + by) % times * count + b) for t in range(times) for a, b in pairs]


def rotated(tiles, by):
    lane = lax.broadcasted_iota(jnp.int32, (SUBLANES, LANES), 1)
    turned = [pltpu.roll(tile, by % LANES, 1) for tile in tiles]
    if len(tiles) == 1:
        return turned
    edge = lane == (0 if by > 0 else LANES - 1)
    return [jnp.where(edge, turned[(w - by) % len(tiles)], turned[w]) for w in range(len(tiles))]


def dlon(tiles):
    return [east - west for east, west in zip(rotated(tiles, -1), rotated(tiles, 1))]


def around(load, q, tiles):
    north = load(q - 1) if q else [pltpu.roll(tile, 1, 0) for tile in load(tiles - 1)]
    south = load(q + 1) if q < tiles - 1 else [pltpu.roll(tile, SUBLANES - 1, 0) for tile in load(0)]
    return north, south


def dlat(load, q, tiles):
    north, south = around(load, q, tiles)
    return [s - n for s, n in zip(south, north)]


def dealt(ref, f, q):
    tiles = ref.shape[-2] // SUBLANES
    return [ref[f, w, pl.ds(q, SUBLANES, stride=tiles), :] for w in range(ref.shape[1])]


def gather_columns(tiles, width):
    lane = lax.broadcasted_iota(jnp.int32, (SUBLANES, LANES), 1)
    packed = jnp.zeros((SUBLANES, LANES), jnp.float32)
    half = LANES // 2
    for f, tile in enumerate(tiles):
        head = pltpu.roll(tile[:, :LANES], half + REACH * f, 1)
        tail = pltpu.roll(tile[:, width - LANES :], REACH * (f + 1), 1)
        at = lane - REACH * f
        packed = jnp.where((at >= 0) & (at < REACH), tail, packed)
        packed = jnp.where((at >= half) & (at < half + REACH), head, packed)
    return packed


def edge_kernel(steps, traj, init, zs_even, zs_odd, sems):
    rows_lat = traj.shape[-2]
    copies = []
    for side, (target, south) in enumerate(((zs_even, False), (zs_odd, True))):
        rows = pl.ds(rows_lat - HALO if south else 0, HALO)
        for l in range(steps + 1):
            source = traj.at[l, :, rows, :] if l < steps else init.at[:, rows, :]
            copies.append(pltpu.make_async_copy(source, target.at[pl.ds(3 * l, 3)], sems.at[side, l]))
    for copy in copies:
        copy.start()
    for copy in copies:
        copy.wait()


def split_kernel(fields, traj, init, own, packs):
    rows_lat, width = traj.shape[-2:]
    for f in range(fields + 3):
        own[f] = traj[f // 3, f % 3] if f < fields else init[f - fields]
    for rows in range(rows_lat // SUBLANES):
        at = pl.ds(rows * SUBLANES, SUBLANES)
        packs[at, :] = gather_columns([own.at[f, at] for f in range(fields + 3)], width)


def other_pack_kernel(fields, *refs):
    own, others, packs = refs[0], refs[1:-1], refs[-1]
    packs[0] = own[...]
    for d in range(len(others) // 3):
        raw, xr_even, xr_odd = others[3 * d : 3 * d + 3]
        rows_lat, width = raw.shape[-2:]
        even = gather_columns([xr_even.at[f] for f in range(fields)], width)
        odd = gather_columns([xr_odd.at[f] for f in range(fields)], width)
        packs[d + 1, :HALO, :] = odd
        packs[d + 1, HALO + rows_lat :, :] = even
        for rows in range(rows_lat // SUBLANES):
            at = pl.ds(rows * SUBLANES, SUBLANES)
            tiles = [raw.at[f // 3, f % 3, at] for f in range(fields)]
            packs[d + 1, pl.ds(HALO + rows * SUBLANES, SUBLANES), :] = gather_columns(tiles, width)


def pack_kernel(fields, packs, zr_even, zr_odd, ys):
    width = zr_even.shape[-1]
    rows_lat = packs.shape[0]
    even = gather_columns([zr_even.at[f] for f in range(fields + 3)], width)
    odd = gather_columns([zr_odd.at[f] for f in range(fields + 3)], width)
    ys[:HALO, :] = odd
    ys[HALO : HALO + rows_lat, :] = packs[...]
    ys[HALO + rows_lat :, :] = even


def place(ext, base, own, even, odd):
    rows_lat, width = own[0].shape
    for f, field in enumerate(own):
        for w in range(width // LANES):
            lanes = pl.ds(w * LANES, LANES)
            ext[base + f, w, pl.ds(HALO, rows_lat), :] = field[:, lanes]
            ext[base + f, w, pl.ds(0, HALO), :] = odd[f, :, lanes]
            ext[base + f, w, pl.ds(rows_lat + HALO, HALO), :] = even[f, :, lanes]


def within(first, count, by=0):
    lane = lax.broadcasted_iota(jnp.int32, (SUBLANES, LANES), 1)
    return (lane - first - by) % LANES < count


def place_strips(strips, ext, count):
    tiles = ext.shape[1]
    for rows in range(ext.shape[2] // SUBLANES):
        rows = pl.ds(rows * SUBLANES, SUBLANES)
        for f in range(count):
            head = pltpu.roll(ext[f, 0, rows, :], LANES // 2 + REACH, 1)
            strips[f, rows, :] = jnp.where(within(LANES // 2 + REACH, 2 * REACH), head, ext[f, tiles - 1, rows, :])


def place_rim(rim, strips, at, count, slot, pack_even, pack_odd):
    half = LANES // 2
    lane = lax.broadcasted_iota(jnp.int32, (SUBLANES, LANES), 1)
    gx_even = lax.axis_index("gx") % 2 == 0
    from_odd = (lane < half) == gx_even
    outside = within(0, REACH) | within(half, REACH)
    for rows in range(strips.shape[1] // SUBLANES):
        rows = pl.ds(rows * SUBLANES, SUBLANES)
        both = jnp.where(from_odd, pack_odd[rows, :], pack_even[rows, :])
        for f in range(count):
            value = pltpu.roll(both, half - REACH * (slot + f), 1)
            rim[at + f, 0, rows, :] = jnp.where(outside, value, strips[at + f, rows, :])


def coriolis(q, rows_lat):
    gy = lax.axis_index("gy")
    nlat = rows_lat * lax.axis_size("gy")
    tiles = (rows_lat + 2 * HALO) // SUBLANES
    row = lax.broadcasted_iota(jnp.int32, (SUBLANES, LANES), 0) * tiles + (q - HALO) + gy * rows_lat
    row = jnp.where(row < 0, row + nlat, jnp.where(row >= nlat, row - nlat, row))
    return CORIOLIS_MEAN + CORIOLIS_SLOPE * ((row.astype(jnp.float32) + 0.5) / nlat - 0.5)


def tendency(load, q, tiles, rotation):
    h, u, v = (load(c, q) for c in range(3))

    def product(at):
        return [b + a * b for a, b in zip(load(0, at), load(2, at))]

    flow = dlon([b + a * b for a, b in zip(h, u)])
    east = [dlon(field) for field in (h, u, v)]
    north = [dlat(functools.partial(load, c), q, tiles) for c in range(3)]
    drift = dlat(product, q, tiles)
    out = ([], [], [])
    for w in range(len(h)):
        out[0].append(h[w] + COURANT * (flow[w] + drift[w]))
        out[1].append(u[w] - rotation * v[w] + COURANT * (east[0][w] + u[w] * east[1][w] + v[w] * north[1][w]))
        out[2].append(v[w] + rotation * u[w] + COURANT * (north[0][w] + u[w] * east[2][w] + v[w] * north[2][w]))
    return out


def horner(rates, weights, state, turn, write):
    outputs, (tiles, across) = range(len(weights)), rates.shape[1:3]

    def blend(n, j, c, q):
        terms = lambda t: (w[j] * rates[3 * i + c, q, t] for i, w in enumerate(weights[n]))
        return [functools.reduce(operator.add, terms(t)) for t in range(across)]

    for q in range(tiles):
        for n in outputs:
            for c in range(3):
                for t, value in enumerate(blend(n, CHEB, c, q)):
                    state[0, n, c, q, t] = value
    for j in range(CHEB - 1, -1, -1):
        now, later = ((CHEB - 1 - j) % 2, (CHEB - j) % 2)
        for q in range(tiles):
            for n in outputs:
                load = lambda c, at, n=n: [state[now, n, c, at, t] for t in range(across)]
                h, u, v = (load(c, q) for c in range(3))
                east_h, east_u = (dlon(h), dlon(u))
                north_h, north_v = (dlat(functools.partial(load, c), q, tiles) for c in (0, 2))
                add = [blend(n, j, c, q) for c in range(3)]
                new = (
                    [add[0][t] + (east_u[t] + north_v[t]) for t in range(across)],
                    [add[1][t] + (east_h[t] - turn[q] * v[t]) for t in range(across)],
                    [add[2][t] + (north_h[t] + turn[q] * u[t]) for t in range(across)],
                )
                for c in range(3):
                    if j:
                        for t in range(across):
                            state[later, n, c, q, t] = new[c][t]
                    else:
                        write(n, c, q, new[c])


def weights_of(lags, lag):
    return [w * CIRCULANT ** (-lag / len(lags)) for w in lags[lag % len(lags)]]


def put(scratch, f, q, values):
    tiles = scratch.shape[-2] // SUBLANES
    for w, value in enumerate(values):
        scratch[f, w, pl.ds(q, SUBLANES, stride=tiles), :] = value


def block_of(scratch, f, rows_lat):
    return jnp.concatenate([scratch[f, w, HALO : HALO + rows_lat] for w in range(scratch.shape[1])], axis=1)


def residuals(times, steps, ext, rates, rotation, write):
    fields, first = 3 * steps, 3 * steps * times
    tiles = rates.shape[1]
    me = lax.axis_index("tm")
    for d in range(times):
        scale = jnp.where(me < d, jnp.float32(CIRCULANT), jnp.float32(1.0))
        for l in range(steps):
            at = d * fields + 3 * l
            before = (at - 3) if l else ((d + 1) % times * fields + fields - 3)
            for q in range(tiles):
                out = tendency(lambda c, row: dealt(ext, at + c, row), q, tiles, rotation[q])
                for c in range(3):
                    prior = dealt(ext, before + c, q)
                    if l == 0:
                        prior = [jnp.where(me == d, a, b) for a, b in zip(dealt(ext, first + c, q), prior)]
                    values = [a - b for a, b in zip(out[c], prior)]
                    if d == 0:
                        write(l, c, q, values)
                    for t, value in enumerate(values):
                        rates[at + c, q, t] = scale * value if d else value


def weights_for(times, steps, lags):
    return [
        [weights_of(lags, d * steps + n - m) for d in range(times) for m in range(steps)] for n in range(steps)
    ]


def block_kernel(times, steps, lags, own, zr_even, zr_odd, *refs):
    fields = 3 * steps
    others = refs[: 3 * (times - 1)]
    strips, part, residual, ext, rates, state, scratch = refs[3 * (times - 1) :]
    rows_lat = own.shape[-2]
    place(ext, 0, [own.at[f] for f in range(fields)], zr_even.at[:fields], zr_odd.at[:fields])
    for d in range(1, times):
        raw, xr_even, xr_odd = others[3 * (d - 1) : 3 * d]
        blocks = [raw.at[f // 3, f % 3] for f in range(fields)]
        place(ext, d * fields, blocks, xr_even, xr_odd)
    place(ext, times * fields, [own.at[fields + c] for c in range(3)], zr_even.at[fields:], zr_odd.at[fields:])
    rotation = [coriolis(q, rows_lat) for q in range(rates.shape[1])]
    residuals(times, steps, ext, rates, rotation, lambda l, c, q, values: put(scratch, 3 * l + c, q, values))
    for l in range(steps):
        for c in range(3):
            residual[l, c] = block_of(scratch, 3 * l + c, rows_lat)
    place_strips(strips, ext, times * fields + 3)
    turn = [r * (1.0 / COURANT) for r in rotation]
    weights = weights_for(times, steps, lags)
    horner(rates, weights, state, turn, lambda n, c, q, values: put(scratch, fields + 3 * n + c, q, values))
    for n in range(steps):
        for c in range(3):
            part[n, c] = block_of(scratch, fields + 3 * n + c, rows_lat)


APART = 4 * REACH


def rim_kernel(times, steps, lags, own, strips, part, part_residual, yr_even, yr_odd, *refs):
    fields, half = 3 * steps, LANES // 2
    updated, residual, rim, rates, state, scratch, ready, sems = refs[times - 1 :]
    rows_lat, width = own.shape[-2:]
    tiles = rates.shape[1]
    place_rim(rim, strips, 0, fields, 0, yr_even.at[0], yr_odd)
    place_rim(rim, strips, times * fields, 3, fields, yr_even.at[0], yr_odd)
    for d in range(1, times):
        place_rim(rim, strips, d * fields, fields, 0, yr_even.at[d], refs[d - 1])
    rotation = [coriolis(q, rows_lat) for q in range(tiles)]
    residuals(times, steps, rim, rates, rotation, lambda l, c, q, values: put(scratch, 3 * l + c, q, values))
    lane = lax.broadcasted_iota(jnp.int32, (rows_lat, LANES), 1)

    def merged(value, strip, by):
        tail = pltpu.roll(strip, LANES - by, 1) if by else strip
        head = pltpu.roll(strip, half - REACH - by, 1)
        value = [value[:, w * LANES : (w + 1) * LANES] for w in range(width // LANES)]
        value[0] = jnp.where(lane < REACH, head, value[0])
        value[-1] = jnp.where(lane >= LANES - REACH, tail, value[-1])
        return jnp.concatenate(value, axis=1)

    copies = []
    for l in range(steps):
        for c in range(3):
            ready[l, c] = merged(part_residual[l, c], block_of(scratch, 3 * l + c, rows_lat), 0)
            copies.append(pltpu.make_async_copy(ready.at[l, c], residual.at[l, c], sems.at[l, c]))
            copies[-1].start()

    second = within(LANES - 2 * REACH, 3 * REACH, APART) | within(half, 3 * REACH, APART)
    for f in range(times * fields):
        for q in range(tiles):
            rates[f, q, 0] = jnp.where(second, pltpu.roll(rates[f, q, 0], APART, 1), rates[f, q, 0])
    turn = [r * (1.0 / COURANT) for r in rotation]
    plain = weights_for(times, steps, lags)
    for n in range(0, steps, 2):
        pair = [
            [[jnp.where(second, b, a) for a, b in zip(*both)] for both in zip(plain[n], plain[min(n + 1, steps - 1)])]
        ]
        horner(rates, pair, state, turn, lambda _, c, q, values: put(scratch, c, q, values))
        for c in range(3):
            strip = block_of(scratch, c, rows_lat)
            for m in range(n, min(n + 2, steps)):
                ready[steps + m, c] = own[3 * m + c] - merged(part[m, c], strip, (m - n) * APART)
                copies.append(pltpu.make_async_copy(ready.at[steps + m, c], updated.at[m, c], sems.at[steps + m, c]))
                copies[-1].start()
    for copy in copies:
        copy.wait()


def step(trajectory, initial):
    steps, _, rows_lat, width = trajectory.shape
    times = lax.axis_size("tm")
    fields = 3 * steps
    lags = polynomials(times * steps)

    def vmem(*shape):
        return pltpu.VMEM(shape, jnp.float32)

    rows, across = (rows_lat + 2 * HALO, width // LANES)
    known = times * fields

    def hbm(*shape):
        return jax.ShapeDtypeStruct(shape, jnp.float32)

    fits = 4 * known * rows * width <= VMEM_KEPT
    near = vmem if fits else hbm

    def kept(*arrays):
        return [pltpu.with_memory_space_constraint(array, pltpu.VMEM) if fits else array for array in arrays]

    zs_even, zs_odd = pl.pallas_call(
        functools.partial(edge_kernel, steps),
        in_specs=[pl.BlockSpec(memory_space=pl.ANY)] * 2,
        out_shape=(near(fields + 3, HALO, width), near(fields + 3, HALO, width)),
        scratch_shapes=[pltpu.SemaphoreType.DMA((2, steps + 1))],
        name="edge_rows",
    )(trajectory, initial)
    count = lax.axis_size("gy")
    zr_odd = lax.ppermute(zs_odd, "gy", [(i, (i + 1) % count) for i in range(count)])
    zr_even = lax.ppermute(zs_even, "gy", [((i + 1) % count, i) for i in range(count)])
    own, packs = pl.pallas_call(
        functools.partial(split_kernel, fields),
        out_shape=(near(fields + 3, rows_lat, width), near(rows_lat, LANES)),
        name="split_block",
    )(trajectory, initial)
    shifts = [[(t, (t + d) % times) for t in range(times)] for d in range(times)]
    raws = [lax.ppermute(trajectory, "tm", shifts[d]) for d in range(1, times)]

    ys = pl.pallas_call(
        functools.partial(pack_kernel, fields),
        out_shape=near(rows, LANES),
        name="pack_edges",
    )(*kept(packs, zr_even, zr_odd))

    even, odd = (pair_up("gx", False), pair_up("gx", True))
    xr_even = [lax.ppermute(zr_even[:fields], "tm", shifts[d]) for d in range(1, times)]
    xr_odd = [lax.ppermute(zr_odd[:fields], "tm", shifts[d]) for d in range(1, times)]
    odds = [lax.ppermute(ys, ("tm", "gx"), with_steps("gx", odd, d)) for d in range(1, times)]
    odds.insert(0, lax.ppermute(ys, "gx", odd))
    known_of = [each for both in zip(raws, xr_even, xr_odd) for each in both]
    ys_all = pl.pallas_call(
        functools.partial(other_pack_kernel, fields),
        out_shape=near(times, rows, LANES),
        name="pack_others",
    )(*kept(ys, *known_of))
    evens = lax.ppermute(ys_all, "gx", even)

    def dealt_out(count, tiles):
        return vmem(count, rows // SUBLANES, tiles, SUBLANES, LANES)

    def working(outputs, scratch, tiles):
        state = vmem(2, outputs, 3, rows // SUBLANES, tiles, SUBLANES, LANES)
        return [dealt_out(known, tiles), state, vmem(scratch, tiles, rows, LANES)]

    strips, part, part_residual = pl.pallas_call(
        functools.partial(block_kernel, times, steps, lags),
        out_shape=(
            near(known + 3, rows, LANES),
            near(steps, 3, rows_lat, width),
            near(steps, 3, rows_lat, width),
        ),
        scratch_shapes=[vmem(known + 3, across, rows, LANES)] + working(steps, 2 * fields, across),
        name="block_part",
    )(*kept(own, zr_even, zr_odd, *known_of))
    updated, residual = pl.pallas_call(
        functools.partial(rim_kernel, times, steps, lags),
        out_shape=(hbm(steps, 3, rows_lat, width), hbm(steps, 3, rows_lat, width)),
        out_specs=(pl.BlockSpec(memory_space=pl.ANY),) * 2,
        scratch_shapes=[
            vmem(known + 3, 1, rows, LANES),
            *working(1, fields, 1),
            vmem(2 * steps, 3, rows_lat, width),
            pltpu.SemaphoreType.DMA((2 * steps, 3)),
        ],
        name="rim_part",
    )(*kept(own, strips, part, part_residual, evens, *odds))
    return updated, residual


def solution(mesh):
    in_specs = (P("tm", None, "gy", "gx"), P(None, "gy", "gx"))
    out_specs = (P("tm", None, "gy", "gx"), P("tm", None, "gy", "gx"))
    return jax.shard_map(step, mesh=mesh, in_specs=in_specs, out_specs=out_specs, check_vma=False)
```
